32 devices in a mesh: grp: 2 (over x), slab: 16 (over z, y, core).
Axes of the slice: x: 2, y: 2, z: 4, core: 2. Of those that a mesh axis runs over, the one named last changes fastest.
Arguments:
- features: bfloat16 [4, 96, 128, 192], P(None, ('grp', 'slab')), parts along dimension 1, may hold values from -6 to 6
- time_cache: bfloat16 [2, 96, 128, 192], P(None, ('grp', 'slab')), parts along dimension 1, may hold values from -6 to 6
- cotangent: bfloat16 [4, 96, 128, 192], P(None, ('grp', 'slab')), parts along dimension 1, may hold values from -6 to 6
- kernel: bfloat16 [3, 3, 3, 192, 192], replicated, may hold values from -0.078125 to 0.078125
- norm_gain: float32 [192], replicated, may hold values from 0.5 to 1.5
- norm_shift: float32 [192], replicated, may hold values from -0.5 to 0.5
- conv_bias: float32 [192], replicated, may hold values from -3 to 3
Outputs:
- decoded: bfloat16 [4, 96, 128, 192], P(None, ('grp', 'slab')), parts along dimension 1
- feature_grad: bfloat16 [4, 96, 128, 192], P(None, 'grp', 'slab'), parts along dimension 1
The draws below stay inside these ranges and needn't reach their ends.
There are 2 independent parts, one for each index of `grp`. The reference program is written for one: setup_inputs(seed, part) draws one part's arguments, and reference() takes and returns one part's arrays. A program takes and returns all parts, laid end to end along the dimension named above; an argument that names none is the same for every part. Nothing has to cross between parts.
All inputs are finite; a program needn't handle non-finite values.
Results may differ from the reference program's by a relative error of at most 0.0029.
Values may be sent and summed in bfloat16 or wider, within the bound.
No kernel may reach another device: no remote copies, remote signals or barrier semaphores. Data moves between devices by JAX's collectives and lax.ppermute only.
A program may use at most 128 MiB of HBM per device.

```python
import jax
import jax.numpy as jnp
from jax import lax

C = 192
FRAMES = 4
COLS = 128
H = 48


def block_levels(stream_key, dims, split, smallest, high):
    def one(position, blocks):
        steps = jax.random.uniform(jax.random.fold_in(jax.random.fold_in(stream_key, 6), position), (blocks,), jnp.float32, smallest / len(split), high / len(split))
        return jnp.repeat(jnp.exp(steps), dims[position] // blocks).reshape((-1,) + (1,) * (len(dims) - position - 1))

    factor_of = one(*split[0])
    for cut in split[1:]:
        factor_of = factor_of * one(*cut)
    return factor_of


def centred(rng, extent, width, most, shards=(), held_as=jnp.bfloat16):
    array = jax.random.normal(rng, extent, jnp.float32) * width
    if len(shards) > 0:
        array = block_levels(rng, extent, shards, -0.22, 0.18) * array
    return jnp.clip(array, min=-most, max=most).astype(held_as)


def setup_inputs(seed: int = 0, part: int = 0) -> dict:
    streams_of = jax.random.split(jax.random.key(seed), 8)
    part_splits = jax.random.split(jax.random.fold_in(streams_of[7], part), 8)
    return {
        "features": centred(part_splits[0], (FRAMES, H, COLS, C), 1.0, 6.0, ((1, 16),)),
        "time_cache": centred(part_splits[1], (2, H, COLS, C), 1.0, 6.0, ((1, 16),)),
        "cotangent": centred(part_splits[2], (FRAMES, H, COLS, C), 1.0, 6.0, ((1, 16),)),
        "kernel": centred(streams_of[3], (3, 3, 3, C, C), (27 * C) ** -0.5, 0.078125),
        "norm_gain": jnp.clip(1.0 + 0.1 * jax.random.normal(streams_of[4], (C,), jnp.float32), 0.5, 1.5),
        "norm_shift": jnp.clip(jax.random.uniform(streams_of[5], (C,), jnp.float32, -0.5, 0.5), -0.5, 0.5),
        "conv_bias": centred(streams_of[6], (C,), 0.5, 3.0, (), jnp.float32),
    }


def convolve(padded, kernel):
    frames = padded.shape[0] - 2
    rows = padded.shape[1] - 2
    cols = padded.shape[2] - 2
    chans = padded.shape[3]
    total = jnp.zeros((frames * rows * cols, kernel.shape[4]), jnp.float32)
    for t in range(3):
        pieces = [padded[t:t + frames, i:i + rows, j:j + cols, :] for i in range(3) for j in range(3)]
        stacked = jnp.concatenate(pieces, axis=-1).reshape(-1, 9 * chans)
        total = total + jnp.dot(stacked, kernel[t].reshape(9 * chans, -1), preferred_element_type=jnp.float32)
    return total.reshape(frames, rows, cols, -1)

def normalize(features, norm_gain, norm_shift):
    values = features.astype(jnp.float32)
    scale = lax.rsqrt(lax.optimization_barrier(jnp.mean(values * values, axis=-1, keepdims=True)) + 1e-06)
    normed = values * scale * norm_gain + norm_shift
    return (values, scale, normed)

def reference(features, time_cache, cotangent, kernel, norm_gain, norm_shift, conv_bias):
    values, scale, normed = normalize(features, norm_gain, norm_shift)
    activated = jax.nn.silu(normed).astype(jnp.bfloat16)
    joined = jnp.concatenate([time_cache, activated], axis=0)
    padded = jnp.pad(joined, ((0, 0), (1, 1), (1, 1), (0, 0)))
    conv = convolve(padded, kernel)
    decoded = (values + conv + conv_bias).astype(jnp.bfloat16)
    flipped = jnp.swapaxes(kernel[::-1, ::-1, ::-1], 3, 4)
    grad_pad = jnp.pad(cotangent, ((0, 2), (1, 1), (1, 1), (0, 0)))
    act_grad = convolve(grad_pad, flipped)
    sig = jax.nn.sigmoid(normed)
    norm_grad = act_grad * sig * (1.0 + normed * (1.0 - sig)) * norm_gain
    inner = lax.optimization_barrier(jnp.mean(norm_grad * values, axis=-1, keepdims=True))
    feature_grad = cotangent.astype(jnp.float32) + scale * norm_grad - values * scale * scale * scale * inner
    return (decoded, feature_grad.astype(jnp.bfloat16))
```

```python
import functools

import jax
import jax.numpy as jnp
from jax import lax
from jax.experimental import pallas as pl
from jax.experimental.pallas import tpu as pltpu
from jax.sharding import PartitionSpec as P

EPS = 1e-06


def column(vector, cols):
    return jnp.transpose(jnp.broadcast_to(vector, (cols, vector.shape[-1])))


def shifted_to(dst, row0, lanes, x, order):
    chans, cols = x.shape
    x32 = x.astype(jnp.float32)
    at = lax.broadcasted_iota(jnp.int32, x.shape, 1)
    for n, s in enumerate(order):
        if s == 0:
            seen = x
        elif s == 1:
            seen = jnp.where(at < cols - 1, pltpu.roll(x32, cols - 1, 1), 0.0)
        else:
            seen = jnp.where(at > 0, pltpu.roll(x32, 1, 1), 0.0)
        dst[row0 + n * chans : row0 + (n + 1) * chans, lanes : lanes + cols] = seen.astype(dst.dtype)


def normalized(x, gain, shift):
    values = x.astype(jnp.float32)
    mean = jnp.sum(values * values, axis=0, keepdims=True) * (1.0 / values.shape[0])
    scale = lax.rsqrt(mean + EPS)
    return values, scale, values * scale * gain + shift


def side_by_side(dst, taps):
    chans = taps[0].shape[0]
    for k in range(0, len(taps), 2):
        pair = taps[k : k + 2]
        dst[:, k * chans : (k + len(pair)) * chans] = pair[0] if len(pair) == 1 else jnp.concatenate(pair, axis=1)


def local_taps(r, rows):
    first = max(r - 1, 0)
    last = min(r + 1, rows - 1)
    return first - (r - 1), last - first + 1, first


def dot(a, b):
    return jnp.dot(a, b, preferred_element_type=jnp.float32)


def grad_sum(lhs_of, stack, lo, hi, frames, cols):
    acc = [None] * frames
    for f0 in range(0, frames, 2):
        for t in range(2, -1, -1):
            g0 = f0 + 2 - t
            count = min(2, frames - g0)
            if count <= 0:
                continue
            part = dot(lhs_of(t), stack[lo:hi, g0 * cols : (g0 + count) * cols])
            for n in range(count):
                piece = part[:, n * cols : (n + 1) * cols]
                acc[f0 + n] = piece if acc[f0 + n] is None else acc[f0 + n] + piece
    return acc


def finish(act_grad, feat, cot, gain, shift):
    values, scale, normed = normalized(feat, gain, shift)
    sig = 1.0 / (1.0 + jnp.exp(-normed))
    norm_grad = act_grad * sig * (1.0 + normed * (1.0 - sig)) * gain
    inner = jnp.sum(norm_grad * values, axis=0, keepdims=True) * (1.0 / values.shape[0])
    return cot.astype(jnp.float32) + scale * norm_grad - values * (scale * scale * scale * inner)


def put_row(out, r, grads, packed):
    frames = len(grads)
    if packed:
        dests = out.shape[0]
        cols = grads[0].shape[1]
        wide = [g[:128] for g in grads]
        for f in range(0, frames, 2):
            wide.append(jnp.concatenate([grads[f][128:], grads[f + 1][128:]], axis=0))
        tiles = [jnp.transpose(w).reshape(dests, cols // dests, 128) for w in wide]
        out[:, r] = jnp.concatenate(tiles, axis=1).astype(jnp.bfloat16)
    else:
        for f in range(frames):
            out[f, r] = jnp.transpose(grads[f]).astype(jnp.bfloat16)


def backward_local_kernel(cot, feat, kern, gain_in, shift_in, out, partial, weights, stack, tail, *, packed):
    frames, rows, chans, cols = cot.shape
    block = 3 * chans
    for t in range(3):
        taps = [kern[t, 2 - d, j] for d in range(3) for j in range(3)]
        side_by_side(weights.at[t], taps)
        side_by_side(tail.at[t], taps[3:])
    for p in range(rows):
        for f in range(frames):
            shifted_to(stack, p * block, f * cols, cot[f, p], (1, 0, -1))
    gain = column(gain_in[...], cols)
    shift = column(shift_in[...], cols)
    edge = 0
    for r in range(rows):
        d0, n, first = local_taps(r, rows)

        def lhs_of(t):
            if d0 == 1:
                return tail[t, :, : n * block]
            return weights[t, :, : n * block]

        acc = grad_sum(lhs_of, stack, first * block, (first + n) * block, frames, cols)
        if n == 3:
            grads = [finish(acc[f], feat[f, r], cot[f, r], gain, shift) for f in range(frames)]
            put_row(out, r, grads, packed)
        else:
            for f in range(frames):
                partial[edge, f] = acc[f]
            edge += 1


def backward_edge_kernel(cot, up, down, feat, partial, weights, before, gain_in, shift_in, out, stack, *, packed):
    frames, rows, chans, cols = cot.shape
    block = 3 * chans
    for f in range(frames):
        shifted_to(stack, 0, f * cols, up[f, 0], (1, 0, -1))
        shifted_to(stack, block, f * cols, down[f, 0], (1, 0, -1))
    gain = column(gain_in[...], cols)
    shift = column(shift_in[...], cols)
    edge = 0
    for r in range(rows):
        if 0 < r < rows - 1:
            if packed:
                out[:, r] = before[:, r]
            else:
                out[:, r] = before[:, r]
            continue
        acc = [partial[edge, f] for f in range(frames)]
        edge += 1
        for d, there in ((0, r == 0), (2, r == rows - 1)):
            if there:
                lo = 0 if d == 0 else block
                more = grad_sum(
                    lambda t: weights[t, :, d * block : (d + 1) * block], stack, lo, lo + block, frames, cols
                )
                acc = [a + b for a, b in zip(acc, more)]
        grads = [finish(acc[f], feat[f, r], cot[f, r], gain, shift) for f in range(frames)]
        put_row(out, r, grads, packed)


def conv_sum(lhs_of, stack, lo, hi, frames, cols):
    acc = []
    for f0 in range(0, frames, 2):
        count = min(2, frames - f0)
        total = None
        for t in range(3):
            part = dot(lhs_of(t), stack[lo:hi, (f0 + t) * cols : (f0 + t + count) * cols])
            total = part if total is None else total + part
        acc += [total[:, n * cols : (n + 1) * cols] for n in range(count)]
    return acc


def activated(x, gain, shift):
    _, _, normed = normalized(x, gain, shift)
    return normed / (1.0 + jnp.exp(-normed))


def forward_local_kernel(feat, cache, kern, gain_in, shift_in, bias_in, out, partial, weights, stack, tail):
    frames, rows, chans, cols = feat.shape
    past = cache.shape[0]
    block = 3 * chans
    gain = column(gain_in[...], cols)
    shift = column(shift_in[...], cols)
    bias = column(bias_in[...], cols)
    for t in range(3):
        whole = jnp.transpose(kern[t].reshape(3 * block, chans))
        weights[t] = whole
        tail[t] = whole[:, block:]
    for p in range(rows):
        for f in range(past):
            shifted_to(stack, p * block, f * cols, cache[f, p], (-1, 0, 1))
        for f in range(frames):
            act = activated(feat[f, p], gain, shift).astype(jnp.bfloat16)
            shifted_to(stack, p * block, (past + f) * cols, act, (-1, 0, 1))
    edge = 0
    for r in range(rows):
        d0, n, first = local_taps(r, rows)

        def lhs_of(t):
            if d0 == 1:
                return tail[t, :, : n * block]
            return weights[t, :, : n * block]

        acc = conv_sum(lhs_of, stack, first * block, (first + n) * block, frames, cols)
        if n == 3:
            for f in range(frames):
                out[f, r] = (feat[f, r].astype(jnp.float32) + acc[f] + bias).astype(jnp.bfloat16)
        else:
            for f in range(frames):
                partial[edge, f] = acc[f]
            edge += 1


def forward_edge_kernel(
    edges, feat, up, down, partial, weights, before, gain_in, shift_in, bias_in, out, stack
):
    frames, rows, chans, cols = feat.shape
    past = up.shape[0] - frames
    block = 3 * chans
    gain = column(gain_in[...], cols)
    shift = column(shift_in[...], cols)
    bias = column(bias_in[...], cols)
    for n, side in enumerate((up, down)):
        for f in range(past):
            shifted_to(stack, n * block, f * cols, side[f, 0], (-1, 0, 1))
        for f in range(past, past + frames):
            act = activated(side[f, 0], gain, shift)
            act = jnp.where(edges[n] > 0, act, 0.0).astype(jnp.bfloat16)
            shifted_to(stack, n * block, f * cols, act, (-1, 0, 1))
    edge = 0
    for r in range(rows):
        if 0 < r < rows - 1:
            out[:, r] = before[:, r]
            continue
        acc = [partial[edge, f] for f in range(frames)]
        edge += 1
        for d, there in ((0, r == 0), (2, r == rows - 1)):
            if there:
                lo = 0 if d == 0 else block
                more = conv_sum(
                    lambda t: weights[t, :, d * block : (d + 1) * block], stack, lo, lo + block, frames, cols
                )
                acc = [a + b for a, b in zip(acc, more)]
        for f in range(frames):
            out[f, r] = (feat[f, r].astype(jnp.float32) + acc[f] + bias).astype(jnp.bfloat16)


def unpack_kernel(src, out):
    frames = out.shape[0]
    for f in range(frames):
        out[f, :, :, :128] = src[:, f * 8 : (f + 1) * 8, :]
        low = (frames + f // 2) * 8
        rest = src[:, low : low + 8, :]
        out[f, :, :, 128:] = rest[:, :, :64] if f % 2 == 0 else rest[:, :, 64:]


VMEM = functools.partial(pl.BlockSpec, memory_space=pltpu.VMEM)
SMEM = functools.partial(pl.BlockSpec, memory_space=pltpu.SMEM)


def call(kernel, name, outs, args, scratch, scalars=0):
    single = not isinstance(outs, list)
    return pl.pallas_call(
        kernel,
        out_shape=outs,
        in_specs=[SMEM()] * scalars + [VMEM()] * (len(args) - scalars),
        out_specs=VMEM() if single else [VMEM()] * len(outs),
        scratch_shapes=[pltpu.VMEM(shape, jnp.bfloat16) for shape in scratch],
        compiler_params=pltpu.CompilerParams(vmem_limit_bytes=24 * 1024 * 1024),
        name=name,
    )(*args)


def body(features, time_cache, cotangent, kernel, norm_gain, norm_shift, conv_bias):
    frames, rows, cols, chans = features.shape
    past = time_cache.shape[0]
    slabs = lax.axis_size("slab")
    index = lax.axis_index("slab")
    up = [(i, i + 1) for i in range(slabs - 1)]
    down = [(i + 1, i) for i in range(slabs - 1)]
    feat = jnp.swapaxes(features, 2, 3)
    cache = jnp.swapaxes(time_cache, 2, 3)
    cot = jnp.swapaxes(cotangent, 2, 3)
    gain = norm_gain.reshape(1, chans)
    shift = norm_shift.reshape(1, chans)
    bias = conv_bias.reshape(1, chans)
    block = 3 * chans
    edge_rows = min(rows, 2)
    per = cols // slabs
    packed = per % 8 == 0 and frames % 2 == 0 and chans == 192
    bf16 = functools.partial(jax.ShapeDtypeStruct, dtype=jnp.bfloat16)
    partial = jax.ShapeDtypeStruct((edge_rows, frames, chans, cols), jnp.float32)
    weights = bf16((3, chans, 3 * block))
    sent = bf16((slabs, rows, frames * per * chans // 128, 128) if packed else (frames, rows, cols, chans))

    cot_up = lax.ppermute(cot[:, rows - 1 :], "slab", up)
    cot_down = lax.ppermute(cot[:, :1], "slab", down)
    grad, part, lhs = call(
        functools.partial(backward_local_kernel, packed=packed),
        "backward_local",
        [sent, partial, weights],
        (cot, feat, kernel, gain, shift),
        [(rows * block, frames * cols), (3, chans, 2 * block)],
    )
    grad = call(
        functools.partial(backward_edge_kernel, packed=packed),
        "backward_edge",
        sent,
        (cot, cot_up, cot_down, feat, part, lhs, grad, gain, shift),
        [(2 * block, frames * cols)],
    )

    if packed:
        moved = lax.all_to_all(grad, "slab", split_axis=0, concat_axis=0, tiled=True)
        moved = moved.reshape(slabs * rows, -1, 128)
        relaid = call(unpack_kernel, "unpack", bf16((frames, slabs * rows, per, chans)), (moved,), [])
    else:
        relaid = lax.all_to_all(grad, "slab", split_axis=2, concat_axis=1, tiled=True)

    feat_b, cache_b, grad = lax.optimization_barrier((feat, cache, grad))
    last = jnp.concatenate([cache_b[:, rows - 1 :], feat_b[:, rows - 1 :]], axis=0)
    first = jnp.concatenate([cache_b[:, :1], feat_b[:, :1]], axis=0)
    above = lax.ppermute(last, "slab", up)
    below = lax.ppermute(first, "slab", down)
    edges = jnp.stack([index, slabs - 1 - index])
    decoded = bf16((frames, rows, chans, cols))
    early, part, lhs = call(
        forward_local_kernel,
        "forward_local",
        [decoded, partial, weights],
        (feat_b, cache_b, kernel, gain, shift, bias),
        [(rows * block, (past + frames) * cols), (3, chans, 2 * block)],
    )
    decoded = call(
        forward_edge_kernel,
        "forward_edge",
        decoded,
        (edges, feat_b, above, below, part, lhs, early, gain, shift, bias),
        [(2 * block, (past + frames) * cols)],
        scalars=1,
    )
    return (jnp.swapaxes(decoded, 2, 3), relaid)


def solution(mesh):
    rows = P(None, ("grp", "slab"), None, None)
    return jax.shard_map(
        body,
        mesh=mesh,
        in_specs=(rows, rows, rows, P(), P(), P(), P()),
        out_specs=(rows, P(None, "grp", "slab", None)),
        check_vma=False,
    )
```

```python
import functools

import jax
import jax.numpy as jnp
from jax import lax
from jax.experimental import pallas as pl
from jax.experimental.pallas import tpu as pltpu
from jax.sharding import PartitionSpec as P

EPS = 1e-06


def column(vector, cols):
    return jnp.transpose(jnp.broadcast_to(vector, (cols, vector.shape[-1])))


def shifted_to(dst, row0, lanes, x, order):
    chans, cols = x.shape
    x32 = x.astype(jnp.float32)
    at = lax.broadcasted_iota(jnp.int32, x.shape, 1)
    for n, s in enumerate(order):
        if s == 0:
            seen = x
        elif s == 1:
            seen = jnp.where(at < cols - 1, pltpu.roll(x32, cols - 1, 1), 0.0)
        else:
            seen = jnp.where(at > 0, pltpu.roll(x32, 1, 1), 0.0)
        dst[row0 + n * chans : row0 + (n + 1) * chans, lanes : lanes + cols] = seen.astype(dst.dtype)


def normalized(x, gain, shift):
    values = x.astype(jnp.float32)
    mean = jnp.sum(values * values, axis=0, keepdims=True) * (1.0 / values.shape[0])
    scale = lax.rsqrt(mean + EPS)
    return values, scale, values * scale * gain + shift


def side_by_side(dst, taps):
    chans = taps[0].shape[0]
    for k in range(0, len(taps), 2):
        pair = taps[k : k + 2]
        dst[:, k * chans : (k + len(pair)) * chans] = pair[0] if len(pair) == 1 else jnp.concatenate(pair, axis=1)


def local_taps(r, rows):
    first = max(r - 1, 0)
    last = min(r + 1, rows - 1)
    return first - (r - 1), last - first + 1, first


def dot(a, b):
    return jnp.dot(a, b, preferred_element_type=jnp.float32)


def grad_sum(lhs_of, stack, lo, hi, frames, cols):
    acc = [None] * frames
    for f0 in range(0, frames, 2):
        for t in range(2, -1, -1):
            g0 = f0 + 2 - t
            count = min(2, frames - g0)
            if count <= 0:
                continue
            part = dot(lhs_of(t), stack[lo:hi, g0 * cols : (g0 + count) * cols])
            for n in range(count):
                piece = part[:, n * cols : (n + 1) * cols]
                acc[f0 + n] = piece if acc[f0 + n] is None else acc[f0 + n] + piece
    return acc


def finish(act_grad, feat, cot, gain, shift):
    values, scale, normed = normalized(feat, gain, shift)
    sig = 1.0 / (1.0 + jnp.exp(-normed))
    norm_grad = act_grad * sig * (1.0 + normed * (1.0 - sig)) * gain
    inner = jnp.sum(norm_grad * values, axis=0, keepdims=True) * (1.0 / values.shape[0])
    return cot.astype(jnp.float32) + scale * norm_grad - values * (scale * scale * scale * inner)


def put_row(out, r, grads, packed):
    frames = len(grads)
    if packed:
        dests = out.shape[0]
        cols = grads[0].shape[1]
        wide = [g[:128] for g in grads]
        for f in range(0, frames, 2):
            wide.append(jnp.concatenate([grads[f][128:], grads[f + 1][128:]], axis=0))
        tiles = [jnp.transpose(w).reshape(dests, cols // dests, 128) for w in wide]
        out[:, r] = jnp.concatenate(tiles, axis=1).astype(jnp.bfloat16)
    else:
        for f in range(frames):
            out[f, r] = jnp.transpose(grads[f]).astype(jnp.bfloat16)


def fetch(pairs, sems):
    copies = [pltpu.make_async_copy(s, d, sems.at[n]) for n, (s, d) in enumerate(pairs)]
    for c in copies:
        c.start()
    return copies


def rows_sent(rows):
    inner = jnp.where(lax.rem(lax.axis_index("slab"), 2) == 0, rows - 1, 0)
    return inner, rows - 1 - inner


def staging_kernel(cot, to_inner, to_outer, sems):
    inner, outer = rows_sent(cot.shape[1])
    for c in fetch([(cot.at[:, inner], to_inner), (cot.at[:, outer], to_outer)], sems):
        c.wait()


def backward_local_kernel(
    cot_hbm, feat_hbm, cache_hbm, kern_hbm, gain_hbm, shift_hbm,
    out, to_inner, to_outer, partial, weights, cot, feat, kern, gain_in, shift_in,
    stack, tail, sent, past_rows, sems, edge_sems, out_sem, *, packed,
):
    frames, rows, chans, cols = cot.shape
    past = cache_hbm.shape[0]
    block = 3 * chans
    edges = list(zip(rows_sent(rows), (to_inner, to_outer)))
    copies = fetch(
        [(cot_hbm, cot), (kern_hbm.at[2], kern.at[2]), (kern_hbm.at[1], kern.at[1]), (kern_hbm.at[0], kern.at[0]),
         (gain_hbm, gain_in), (shift_hbm, shift_in), (feat_hbm, feat)]
        + [(cache_hbm.at[:, row], past_rows.at[n]) for n, (row, _) in enumerate(edges)],
        sems,
    )
    copies[0].wait()
    for p in range(rows):
        for f in range(frames):
            shifted_to(stack, p * block, f * cols, cot[f, p], (1, 0, -1))
    for n, t in ((1, 2), (2, 1), (3, 0)):
        copies[n].wait()
        taps = [kern[t, 2 - d, j] for d in range(3) for j in range(3)]
        side_by_side(weights.at[t], taps)
        side_by_side(tail.at[t], taps[3:])
    for c in copies[4:]:
        c.wait()
    written = fetch(
        [(feat.at[:, row], to.at[pl.ds(past, frames)]) for row, to in edges]
        + [(past_rows.at[n], to.at[pl.ds(0, past)]) for n, (_, to) in enumerate(edges)],
        edge_sems,
    )
    gain = column(gain_in[...], cols)
    shift = column(shift_in[...], cols)
    for r in list(range(1, rows - 1)) + sorted({0, rows - 1}):
        d0, n, first = local_taps(r, rows)

        def lhs_of(t):
            if d0 == 1:
                return tail[t, :, : n * block]
            return weights[t, :, : n * block]

        acc = grad_sum(lhs_of, stack, first * block, (first + n) * block, frames, cols)
        if n == 3:
            grads = [finish(acc[f], feat[f, r], cot[f, r], gain, shift) for f in range(frames)]
            put_row(sent, r - 1, grads, packed)
            written.append(pltpu.make_async_copy(sent.at[:, r - 1], out.at[:, r], out_sem.at[r - 1]))
            written[-1].start()
        else:
            for f in range(frames):
                partial[min(r, 1), f] = acc[f]
    for c in written:
        c.wait()


def backward_edge_kernel(
    cot, inner, outer, feat, partial, weights, gain_in, shift_in, before, out, stack, sent, out_sem, *, packed
):
    del before
    frames, rows, chans, cols = cot.shape
    block = 3 * chans
    slot = jnp.where(lax.rem(lax.axis_index("slab"), 2) == 0, 1, 0)
    for f in range(frames):
        shifted_to(stack.at[slot], 0, f * cols, inner[f], (1, 0, -1))
        shifted_to(stack.at[1 - slot], 0, f * cols, outer[f], (1, 0, -1))
    gain = column(gain_in[...], cols)
    shift = column(shift_in[...], cols)
    written = []
    for edge, r in enumerate(sorted({0, rows - 1})):
        acc = [partial[edge, f] for f in range(frames)]
        for d, there in ((0, r == 0), (2, r == rows - 1)):
            if there:
                more = grad_sum(
                    lambda t: weights[t, :, d * block : (d + 1) * block], stack.at[d // 2], 0, block, frames, cols
                )
                acc = [a + b for a, b in zip(acc, more)]
        grads = [finish(acc[f], feat[f, r], cot[f, r], gain, shift) for f in range(frames)]
        put_row(sent, edge, grads, packed)
        written.append(pltpu.make_async_copy(sent.at[:, edge], out.at[:, r], out_sem.at[edge]))
        written[-1].start()
    for c in written:
        c.wait()


def conv_sum(lhs_of, stack, lo, hi, frames, cols):
    acc = []
    for f0 in range(0, frames, 2):
        count = min(2, frames - f0)
        total = None
        for t in range(3):
            part = dot(lhs_of(t), stack[lo:hi, (f0 + t) * cols : (f0 + t + count) * cols])
            total = part if total is None else total + part
        acc += [total[:, n * cols : (n + 1) * cols] for n in range(count)]
    return acc


def activated(x, gain, shift):
    _, _, normed = normalized(x, gain, shift)
    return normed / (1.0 + jnp.exp(-normed))


def forward_local_kernel(
    feat, cache, kern, gain_in, shift_in, bias_in, out, partial, weights, stack, tail, ready, out_sem
):
    frames, rows, chans, cols = feat.shape
    past = cache.shape[0]
    block = 3 * chans
    gain = column(gain_in[...], cols)
    shift = column(shift_in[...], cols)
    bias = column(bias_in[...], cols)
    for t in range(3):
        whole = jnp.transpose(kern[t].reshape(3 * block, chans))
        weights[t] = whole
        tail[t] = whole[:, block:]
    for p in range(rows):
        for f in range(past):
            shifted_to(stack, p * block, f * cols, cache[f, p], (-1, 0, 1))
        for f in range(frames):
            act = activated(feat[f, p], gain, shift).astype(jnp.bfloat16)
            shifted_to(stack, p * block, (past + f) * cols, act, (-1, 0, 1))
    written = []
    for r in list(range(1, rows - 1)) + sorted({0, rows - 1}):
        d0, n, first = local_taps(r, rows)

        def lhs_of(t):
            if d0 == 1:
                return tail[t, :, : n * block]
            return weights[t, :, : n * block]

        acc = conv_sum(lhs_of, stack, first * block, (first + n) * block, frames, cols)
        decoded = [feat[f, r].astype(jnp.float32) + acc[f] + bias for f in range(frames)]
        if n == 3:
            for f in range(frames):
                ready[f, r - 1] = decoded[f].astype(jnp.bfloat16)
            written.append(pltpu.make_async_copy(ready.at[:, r - 1], out.at[:, r], out_sem.at[r - 1]))
            written[-1].start()
        else:
            for f in range(frames):
                partial[min(r, 1), f] = decoded[f]
    for c in written:
        c.wait()


def forward_edge_kernel(
    inner_hbm, outer_hbm, partial, weights, gain_in, shift_in, before, out, inner, outer, stack, ready, sems, out_sem
):
    del before
    rows = out.shape[1]
    frames, chans, cols = partial.shape[1:]
    past = inner.shape[0] - frames
    block = 3 * chans
    arriving = fetch([(inner_hbm, inner), (outer_hbm, outer)], sems)
    index = lax.axis_index("slab")
    slot = jnp.where(lax.rem(index, 2) == 0, 1, 0)
    inside = jnp.logical_and(index > 0, index < lax.axis_size("slab") - 1)
    gain = column(gain_in[...], cols)
    shift = column(shift_in[...], cols)
    for n, (side, to, held) in enumerate(((inner, slot, None), (outer, 1 - slot, inside))):
        arriving[n].wait()
        for f in range(past):
            shifted_to(stack.at[to], 0, f * cols, side[f], (-1, 0, 1))
        for f in range(past, past + frames):
            act = activated(side[f], gain, shift)
            if held is not None:
                act = jnp.where(held, act, 0.0)
            shifted_to(stack.at[to], 0, f * cols, act.astype(jnp.bfloat16), (-1, 0, 1))
    written = []
    for edge, r in enumerate(sorted({0, rows - 1})):
        acc = [partial[edge, f] for f in range(frames)]
        for d, there in ((0, r == 0), (2, r == rows - 1)):
            if there:
                more = conv_sum(
                    lambda t: weights[t, :, d * block : (d + 1) * block], stack.at[d // 2], 0, block, frames, cols
                )
                acc = [a + b for a, b in zip(acc, more)]
        for f in range(frames):
            ready[f, edge] = acc[f].astype(jnp.bfloat16)
        written.append(pltpu.make_async_copy(ready.at[:, edge], out.at[:, r], out_sem.at[edge]))
        written[-1].start()
    for c in written:
        c.wait()


def unpack_kernel(src_hbm, out_hbm, src, out, in_sem, out_sem):
    frames, lines = out.shape[:2]
    parts = in_sem.shape[0]
    step = lines // parts
    spans = [pl.ds(n * step, step) for n in range(parts)]
    arriving = fetch([(src_hbm.at[s], src.at[s]) for s in spans], in_sem)
    leaving = [pltpu.make_async_copy(out.at[:, s], out_hbm.at[:, s], out_sem.at[n]) for n, s in enumerate(spans)]
    for n, s in enumerate(spans):
        arriving[n].wait()
        for f in range(frames):
            out[f, s, :, :128] = src[s, f * 8 : (f + 1) * 8, :]
            low = (frames + f // 2) * 8
            rest = src[s, low : low + 8, :]
            out[f, s, :, 128:] = rest[:, :, :64] if f % 2 == 0 else rest[:, :, 64:]
        leaving[n].start()
    for c in leaving:
        c.wait()


VMEM = functools.partial(pl.BlockSpec, memory_space=pltpu.VMEM)
HBM = functools.partial(pl.BlockSpec, memory_space=pltpu.HBM)


def call(kernel, name, ins, outs, scratch=(), aliases=None):
    result = pl.pallas_call(
        kernel,
        out_shape=[pltpu.HBM(o.shape, o.dtype) if where is HBM else o for o, where in outs],
        in_specs=[where() for _, where in ins],
        out_specs=[where() for _, where in outs],
        scratch_shapes=list(scratch),
        input_output_aliases=aliases or {},
        compiler_params=pltpu.CompilerParams(vmem_limit_bytes=24 * 1024 * 1024),
        name=name,
    )(*[pltpu.with_memory_space_constraint(a, pltpu.HBM) if where is HBM else a for a, where in ins])
    return result[0] if len(outs) == 1 else result


def body(features, time_cache, cotangent, kernel, norm_gain, norm_shift, conv_bias):
    frames, rows, cols, chans = features.shape
    past = time_cache.shape[0]
    slabs = lax.axis_size("slab")
    within = [(i, i ^ 1) for i in range(slabs)]
    across = [(i, i + 1) for i in range(1, slabs - 1, 2)] + [(i + 1, i) for i in range(1, slabs - 1, 2)]
    feat = jnp.swapaxes(features, 2, 3)
    cache = jnp.swapaxes(time_cache, 2, 3)
    cot = jnp.swapaxes(cotangent, 2, 3)
    gain = norm_gain.reshape(1, chans)
    shift = norm_shift.reshape(1, chans)
    bias = conv_bias.reshape(1, chans)
    block = 3 * chans
    edge_rows = min(rows, 2)
    per = cols // slabs
    packed = per % 8 == 0 and frames % 2 == 0 and chans == 192
    bf16 = functools.partial(jax.ShapeDtypeStruct, dtype=jnp.bfloat16)
    vmem16 = functools.partial(pltpu.VMEM, dtype=jnp.bfloat16)
    partial = jax.ShapeDtypeStruct((edge_rows, frames, chans, cols), jnp.float32)
    weights = bf16((3, chans, 3 * block))

    def sent(n):
        return (slabs, n, frames * per * chans // 128, 128) if packed else (frames, n, cols, chans)

    cot_in, cot_across = call(
        staging_kernel,
        "staging",
        [(cot, HBM)],
        [(bf16((frames, chans, cols)), VMEM)] * 2,
        [pltpu.SemaphoreType.DMA((2,))],
    )
    cot_in = lax.ppermute(cot_in, "slab", within)
    cot_across = lax.ppermute(cot_across, "slab", across)
    grad, act_in, act_across, part, lhs, cot_v, feat_v, kern_v, gain_v, shift_v = call(
        functools.partial(backward_local_kernel, packed=packed),
        "backward_local",
        [(a, HBM) for a in (cot, feat, cache, kernel, gain, shift)],
        [(bf16(sent(rows)), HBM)]
        + [(bf16((past + frames, chans, cols)), HBM)] * 2
        + [(partial, VMEM), (weights, VMEM)]
        + [(jax.ShapeDtypeStruct(a.shape, a.dtype), VMEM) for a in (cot, feat, kernel, gain, shift)],
        [
            vmem16((rows * block, frames * cols)),
            vmem16((3, chans, 2 * block)),
            vmem16(sent(max(rows - 2, 1))),
            vmem16((2, past, chans, cols)),
            pltpu.SemaphoreType.DMA((9,)),
            pltpu.SemaphoreType.DMA((4,)),
            pltpu.SemaphoreType.DMA((max(rows - 2, 1),)),
        ],
    )
    grad = call(
        functools.partial(backward_edge_kernel, packed=packed),
        "backward_edge",
        [(a, VMEM) for a in (cot_v, cot_in, cot_across, feat_v, part, lhs, gain_v, shift_v)] + [(grad, HBM)],
        [(bf16(sent(rows)), HBM)],
        [vmem16((2, block, frames * cols)), vmem16(sent(edge_rows)), pltpu.SemaphoreType.DMA((edge_rows,))],
        aliases={8: 0},
    )

    if packed:
        moved = lax.all_to_all(grad, "slab", split_axis=0, concat_axis=0, tiled=True)
        moved = moved.reshape(slabs * rows, -1, 128)
        relaid = (frames, slabs * rows, per, chans)
        parts = 4 if slabs * rows % 4 == 0 else 1
        relaid = call(
            unpack_kernel,
            "unpack",
            [(moved, HBM)],
            [(bf16(relaid), HBM)],
            [vmem16(moved.shape), vmem16(relaid), pltpu.SemaphoreType.DMA((parts,)), pltpu.SemaphoreType.DMA((parts,))],
        )
    else:
        relaid = lax.all_to_all(grad, "slab", split_axis=2, concat_axis=1, tiled=True)

    act_in, act_across, feat_v, kern_v, gain_v, shift_v, _ = lax.optimization_barrier(
        (act_in, act_across, feat_v, kern_v, gain_v, shift_v, grad)
    )
    act_in = lax.ppermute(act_in, "slab", within)
    act_across = lax.ppermute(act_across, "slab", across)
    decoded, part, lhs = call(
        forward_local_kernel,
        "forward_local",
        [(a, VMEM) for a in (feat_v, cache, kern_v, gain_v, shift_v, bias)],
        [(bf16((frames, rows, chans, cols)), HBM), (partial, VMEM), (weights, VMEM)],
        [
            vmem16((rows * block, (past + frames) * cols)),
            vmem16((3, chans, 2 * block)),
            vmem16((frames, max(rows - 2, 1), chans, cols)),
            pltpu.SemaphoreType.DMA((max(rows - 2, 1),)),
        ],
    )
    decoded = call(
        forward_edge_kernel,
        "forward_edge",
        [(act_in, HBM), (act_across, HBM)] + [(a, VMEM) for a in (part, lhs, gain_v, shift_v)] + [(decoded, HBM)],
        [(bf16((frames, rows, chans, cols)), HBM)],
        [
            vmem16((past + frames, chans, cols)),
            vmem16((past + frames, chans, cols)),
            vmem16((2, block, (past + frames) * cols)),
            vmem16((frames, edge_rows, chans, cols)),
            pltpu.SemaphoreType.DMA((2,)),
            pltpu.SemaphoreType.DMA((edge_rows,)),
        ],
        aliases={6: 0},
    )
    return (jnp.swapaxes(decoded, 2, 3), relaid)


def solution(mesh):
    rows = P(None, ("grp", "slab"), None, None)
    return jax.shard_map(
        body,
        mesh=mesh,
        in_specs=(rows, rows, rows, P(), P(), P(), P()),
        out_specs=(rows, P(None, "grp", "slab", None)),
        check_vma=False,
    )
```

```python
import functools

import jax
import jax.numpy as jnp
from jax import lax
from jax.experimental import pallas as pl
from jax.experimental.pallas import tpu as pltpu
from jax.sharding import PartitionSpec as P

EPS = 1e-06
HINT = 10**10


def column(vector, cols):
    return jnp.transpose(jnp.broadcast_to(vector, (cols, vector.shape[-1])))


def shifted_to(dst, row0, lanes, x, order):
    chans, cols = x.shape
    x32 = x.astype(jnp.float32)
    at = lax.broadcasted_iota(jnp.int32, x.shape, 1)
    for n, s in enumerate(order):
        if s == 0:
            seen = x
        elif s == 1:
            seen = jnp.where(at < cols - 1, pltpu.roll(x32, cols - 1, 1), 0.0)
        else:
            seen = jnp.where(at > 0, pltpu.roll(x32, 1, 1), 0.0)
        dst[row0 + n * chans : row0 + (n + 1) * chans, lanes : lanes + cols] = seen.astype(dst.dtype)


def normalized(x, gain, shift):
    values = x.astype(jnp.float32)
    mean = jnp.sum(values * values, axis=0, keepdims=True) * (1.0 / values.shape[0])
    scale = lax.rsqrt(mean + EPS)
    return values, scale, values * scale * gain + shift


def side_by_side(dst, taps):
    chans = taps[0].shape[0]
    for k in range(0, len(taps), 2):
        pair = taps[k : k + 2]
        dst[:, k * chans : (k + len(pair)) * chans] = pair[0] if len(pair) == 1 else jnp.concatenate(pair, axis=1)


def local_taps(r, rows):
    first = max(r - 1, 0)
    last = min(r + 1, rows - 1)
    return first - (r - 1), last - first + 1, first


def dot(a, b):
    return jnp.dot(a, b, preferred_element_type=jnp.float32)


def grad_sum(lhs_of, stack, lo, hi, frames, cols):
    acc = [None] * frames
    for f0 in range(0, frames, 2):
        for t in range(2, -1, -1):
            g0 = f0 + 2 - t
            count = min(2, frames - g0)
            if count <= 0:
                continue
            part = dot(lhs_of(t), stack[lo:hi, g0 * cols : (g0 + count) * cols])
            for n in range(count):
                piece = part[:, n * cols : (n + 1) * cols]
                acc[f0 + n] = piece if acc[f0 + n] is None else acc[f0 + n] + piece
    return acc


def finish(act_grad, feat, cot, gain, shift):
    values, scale, normed = normalized(feat, gain, shift)
    sig = 1.0 / (1.0 + jnp.exp(-normed))
    norm_grad = act_grad * sig * (1.0 + normed * (1.0 - sig)) * gain
    inner = jnp.sum(norm_grad * values, axis=0, keepdims=True) * (1.0 / values.shape[0])
    return cot.astype(jnp.float32) + scale * norm_grad - values * (scale * scale * scale * inner)


def put_row(out, r, grads, packed):
    frames = len(grads)
    if packed:
        dests = out.shape[0]
        cols = grads[0].shape[1]
        wide = [g[:128] for g in grads]
        for f in range(0, frames, 2):
            wide.append(jnp.concatenate([grads[f][128:], grads[f + 1][128:]], axis=0))
        tiles = [jnp.transpose(w).reshape(dests, cols // dests, 128) for w in wide]
        out[:, r] = jnp.concatenate(tiles, axis=1).astype(jnp.bfloat16)
    else:
        for f in range(frames):
            out[f, r] = jnp.transpose(grads[f]).astype(jnp.bfloat16)


def fetch(pairs, sems):
    copies = [pltpu.make_async_copy(s, d, sems.at[n]) for n, (s, d) in enumerate(pairs)]
    for c in copies:
        c.start()
    return copies


def rows_sent(rows):
    inner = jnp.where(lax.rem(lax.axis_index("slab"), 2) == 0, rows - 1, 0)
    return inner, rows - 1 - inner


def staging_kernel(cot, to_inner, to_outer, sems):
    inner, outer = rows_sent(cot.shape[1])
    for c in fetch([(cot.at[:, inner], to_inner), (cot.at[:, outer], to_outer)], sems):
        c.wait()


def backward_local_kernel(
    cot_hbm, feat_hbm, cache_hbm, kern_hbm, gain_hbm, shift_hbm,
    out, to_inner, to_outer, partial, weights, cot, feat, kern, gain_in, shift_in,
    stack, tail, sent, past_rows, sems, edge_sems, out_sem, *, packed,
):
    frames, rows, chans, cols = cot.shape
    past = cache_hbm.shape[0]
    block = 3 * chans
    edges = list(zip(rows_sent(rows), (to_inner, to_outer)))
    copies = fetch(
        [(cot_hbm, cot), (kern_hbm.at[2], kern.at[2]), (kern_hbm.at[1], kern.at[1]), (kern_hbm.at[0], kern.at[0]),
         (gain_hbm, gain_in), (shift_hbm, shift_in), (feat_hbm, feat)]
        + [(cache_hbm.at[:, row], past_rows.at[n]) for n, (row, _) in enumerate(edges)],
        sems,
    )
    copies[0].wait()
    for p in range(rows):
        for f in range(frames):
            shifted_to(stack, p * block, f * cols, cot[f, p], (1, 0, -1))
    for n, t in ((1, 2), (2, 1), (3, 0)):
        copies[n].wait()
        taps = [kern[t, 2 - d, j] for d in range(3) for j in range(3)]
        side_by_side(weights.at[t], taps)
        side_by_side(tail.at[t], taps[3:])
    for c in copies[4:]:
        c.wait()
    written = fetch(
        [(feat.at[:, row], to.at[pl.ds(past, frames)]) for row, to in edges]
        + [(past_rows.at[n], to.at[pl.ds(0, past)]) for n, (_, to) in enumerate(edges)],
        edge_sems,
    )
    gain = column(gain_in[...], cols)
    shift = column(shift_in[...], cols)
    for r in list(range(1, rows - 1)) + sorted({0, rows - 1}):
        d0, n, first = local_taps(r, rows)

        def lhs_of(t):
            if d0 == 1:
                return tail[t, :, : n * block]
            return weights[t, :, : n * block]

        acc = grad_sum(lhs_of, stack, first * block, (first + n) * block, frames, cols)
        if n == 3:
            grads = [finish(acc[f], feat[f, r], cot[f, r], gain, shift) for f in range(frames)]
            put_row(sent, r - 1, grads, packed)
            written.append(pltpu.make_async_copy(sent.at[:, r - 1], out.at[:, r], out_sem.at[r - 1]))
            written[-1].start()
        else:
            for f in range(frames):
                partial[min(r, 1), f] = acc[f]
    for c in written:
        c.wait()


def backward_edge_kernel(
    cot, inner, outer, feat, partial, weights, gain_in, shift_in, before, out, stack, sent, out_sem, *, packed
):
    del before
    frames, rows, chans, cols = cot.shape
    block = 3 * chans
    slot = jnp.where(lax.rem(lax.axis_index("slab"), 2) == 0, 1, 0)
    for f in range(frames):
        shifted_to(stack.at[slot], 0, f * cols, inner[f], (1, 0, -1))
        shifted_to(stack.at[1 - slot], 0, f * cols, outer[f], (1, 0, -1))
    gain = column(gain_in[...], cols)
    shift = column(shift_in[...], cols)
    written = []
    for edge, r in enumerate(sorted({0, rows - 1})):
        acc = [partial[edge, f] for f in range(frames)]
        for d, there in ((0, r == 0), (2, r == rows - 1)):
            if there:
                more = grad_sum(
                    lambda t: weights[t, :, d * block : (d + 1) * block], stack.at[d // 2], 0, block, frames, cols
                )
                acc = [a + b for a, b in zip(acc, more)]
        grads = [finish(acc[f], feat[f, r], cot[f, r], gain, shift) for f in range(frames)]
        put_row(sent, edge, grads, packed)
        written.append(pltpu.make_async_copy(sent.at[:, edge], out.at[:, r], out_sem.at[edge]))
        written[-1].start()
    for c in written:
        c.wait()


def conv_sum(lhs_of, stack, lo, hi, frames, cols):
    acc = []
    for f0 in range(0, frames, 2):
        count = min(2, frames - f0)
        total = None
        for t in range(3):
            part = dot(lhs_of(t), stack[lo:hi, (f0 + t) * cols : (f0 + t + count) * cols])
            total = part if total is None else total + part
        acc += [total[:, n * cols : (n + 1) * cols] for n in range(count)]
    return acc


def activated(x, gain, shift):
    _, _, normed = normalized(x, gain, shift)
    return normed / (1.0 + jnp.exp(-normed))


def forward_local_kernel(
    feat, cache, kern, gain_in, shift_in, bias_in, out, partial, weights, stack, tail, ready, out_sem
):
    frames, rows, chans, cols = feat.shape
    past = cache.shape[0]
    block = 3 * chans
    gain = column(gain_in[...], cols)
    shift = column(shift_in[...], cols)
    bias = column(bias_in[...], cols)
    for t in range(3):
        whole = jnp.transpose(kern[t].reshape(3 * block, chans))
        weights[t] = whole
        tail[t] = whole[:, block:]
    for p in range(rows):
        for f in range(past):
            shifted_to(stack, p * block, f * cols, cache[f, p], (-1, 0, 1))
        for f in range(frames):
            act = activated(feat[f, p], gain, shift).astype(jnp.bfloat16)
            shifted_to(stack, p * block, (past + f) * cols, act, (-1, 0, 1))
    written = []
    for r in list(range(1, rows - 1)) + sorted({0, rows - 1}):
        d0, n, first = local_taps(r, rows)

        def lhs_of(t):
            if d0 == 1:
                return tail[t, :, : n * block]
            return weights[t, :, : n * block]

        acc = conv_sum(lhs_of, stack, first * block, (first + n) * block, frames, cols)
        decoded = [feat[f, r].astype(jnp.float32) + acc[f] + bias for f in range(frames)]
        if n == 3:
            for f in range(frames):
                ready[f, r - 1] = decoded[f].astype(jnp.bfloat16)
            written.append(pltpu.make_async_copy(ready.at[:, r - 1], out.at[:, r], out_sem.at[r - 1]))
            written[-1].start()
        else:
            for f in range(frames):
                partial[min(r, 1), f] = decoded[f]
    for c in written:
        c.wait()


def forward_edge_kernel(
    inner_hbm, outer_hbm, partial, weights, gain_in, shift_in, before, out, inner, outer, stack, ready, sems, out_sem
):
    del before
    rows = out.shape[1]
    frames, chans, cols = partial.shape[1:]
    past = inner.shape[0] - frames
    block = 3 * chans
    arriving = fetch([(inner_hbm, inner), (outer_hbm, outer)], sems)
    index = lax.axis_index("slab")
    slot = jnp.where(lax.rem(index, 2) == 0, 1, 0)
    inside = jnp.logical_and(index > 0, index < lax.axis_size("slab") - 1)
    gain = column(gain_in[...], cols)
    shift = column(shift_in[...], cols)
    for n, (side, to, held) in enumerate(((inner, slot, None), (outer, 1 - slot, inside))):
        arriving[n].wait()
        for f in range(past):
            shifted_to(stack.at[to], 0, f * cols, side[f], (-1, 0, 1))
        for f in range(past, past + frames):
            act = activated(side[f], gain, shift)
            if held is not None:
                act = jnp.where(held, act, 0.0)
            shifted_to(stack.at[to], 0, f * cols, act.astype(jnp.bfloat16), (-1, 0, 1))
    written = []
    for edge, r in enumerate(sorted({0, rows - 1})):
        acc = [partial[edge, f] for f in range(frames)]
        for d, there in ((0, r == 0), (2, r == rows - 1)):
            if there:
                more = conv_sum(
                    lambda t: weights[t, :, d * block : (d + 1) * block], stack.at[d // 2], 0, block, frames, cols
                )
                acc = [a + b for a, b in zip(acc, more)]
        for f in range(frames):
            ready[f, edge] = acc[f].astype(jnp.bfloat16)
        written.append(pltpu.make_async_copy(ready.at[:, edge], out.at[:, r], out_sem.at[edge]))
        written[-1].start()
    for c in written:
        c.wait()


def unpack_kernel(src_hbm, out_hbm, src, out, in_sem, out_sem):
    frames, lines = out.shape[:2]
    parts = in_sem.shape[0]
    step = lines // parts
    spans = [pl.ds(n * step, step) for n in range(parts)]
    arriving = fetch([(src_hbm.at[s], src.at[s]) for s in spans], in_sem)
    leaving = [pltpu.make_async_copy(out.at[:, s], out_hbm.at[:, s], out_sem.at[n]) for n, s in enumerate(spans)]
    for n, s in enumerate(spans):
        arriving[n].wait()
        for f in range(frames):
            out[f, s, :, :128] = src[s, f * 8 : (f + 1) * 8, :]
            low = (frames + f // 2) * 8
            rest = src[s, low : low + 8, :]
            out[f, s, :, 128:] = rest[:, :, :64] if f % 2 == 0 else rest[:, :, 64:]
        leaving[n].start()
    for c in leaving:
        c.wait()


VMEM = functools.partial(pl.BlockSpec, memory_space=pltpu.VMEM)
HBM = functools.partial(pl.BlockSpec, memory_space=pltpu.HBM)


def call(kernel, name, ins, outs, scratch=(), aliases=None, flops=None):
    result = pl.pallas_call(
        kernel,
        out_shape=[pltpu.HBM(o.shape, o.dtype) if where is HBM else o for o, where in outs],
        in_specs=[where() for _, where in ins],
        out_specs=[where() for _, where in outs],
        scratch_shapes=list(scratch),
        input_output_aliases=aliases or {},
        compiler_params=pltpu.CompilerParams(vmem_limit_bytes=24 * 1024 * 1024),
        cost_estimate=flops and pl.CostEstimate(flops=flops, transcendentals=0, bytes_accessed=0),
        name=name,
    )(*[pltpu.with_memory_space_constraint(a, pltpu.HBM) if where is HBM else a for a, where in ins])
    return result[0] if len(outs) == 1 else result


def body(features, time_cache, cotangent, kernel, norm_gain, norm_shift, conv_bias):
    frames, rows, cols, chans = features.shape
    past = time_cache.shape[0]
    slabs = lax.axis_size("slab")
    within = [(i, i ^ 1) for i in range(slabs)]
    across = [(i, i + 1) for i in range(1, slabs - 1, 2)] + [(i + 1, i) for i in range(1, slabs - 1, 2)]
    feat = jnp.swapaxes(features, 2, 3)
    cache = jnp.swapaxes(time_cache, 2, 3)
    cot = jnp.swapaxes(cotangent, 2, 3)
    gain = norm_gain.reshape(1, chans)
    shift = norm_shift.reshape(1, chans)
    bias = conv_bias.reshape(1, chans)
    block = 3 * chans
    edge_rows = min(rows, 2)
    per = cols // slabs
    packed = per % 8 == 0 and frames % 2 == 0 and chans == 192
    bf16 = functools.partial(jax.ShapeDtypeStruct, dtype=jnp.bfloat16)
    vmem16 = functools.partial(pltpu.VMEM, dtype=jnp.bfloat16)
    partial = jax.ShapeDtypeStruct((edge_rows, frames, chans, cols), jnp.float32)
    weights = bf16((3, chans, 3 * block))

    def sent(n):
        return (slabs, n, frames * per * chans // 128, 128) if packed else (frames, n, cols, chans)

    cot_in, cot_across = call(
        staging_kernel,
        "staging",
        [(cot, HBM)],
        [(bf16((frames, chans, cols)), VMEM)] * 2,
        [pltpu.SemaphoreType.DMA((2,))],
    )
    cot_in = lax.ppermute(cot_in, "slab", within)
    cot_across = lax.ppermute(cot_across, "slab", across)
    grad, act_in, act_across, part, lhs, cot_v, feat_v, kern_v, gain_v, shift_v = call(
        functools.partial(backward_local_kernel, packed=packed),
        "backward_local",
        [(a, HBM) for a in (cot, feat, cache, kernel, gain, shift)],
        [(bf16(sent(rows)), HBM)]
        + [(bf16((past + frames, chans, cols)), HBM)] * 2
        + [(partial, VMEM), (weights, VMEM)]
        + [(jax.ShapeDtypeStruct(a.shape, a.dtype), VMEM) for a in (cot, feat, kernel, gain, shift)],
        [
            vmem16((rows * block, frames * cols)),
            vmem16((3, chans, 2 * block)),
            vmem16(sent(max(rows - 2, 1))),
            vmem16((2, past, chans, cols)),
            pltpu.SemaphoreType.DMA((9,)),
            pltpu.SemaphoreType.DMA((4,)),
            pltpu.SemaphoreType.DMA((max(rows - 2, 1),)),
        ],
    )
    act_in = lax.ppermute(act_in, "slab", within)
    act_across = lax.ppermute(act_across, "slab", across)
    grad = call(
        functools.partial(backward_edge_kernel, packed=packed),
        "backward_edge",
        [(a, VMEM) for a in (cot_v, cot_in, cot_across, feat_v, part, lhs, gain_v, shift_v)] + [(grad, HBM)],
        [(bf16(sent(rows)), HBM)],
        [vmem16((2, block, frames * cols)), vmem16(sent(edge_rows)), pltpu.SemaphoreType.DMA((edge_rows,))],
        aliases={8: 0},
    )

    if packed:
        moved = lax.all_to_all(grad, "slab", split_axis=0, concat_axis=0, tiled=True)
        moved = moved.reshape(slabs * rows, -1, 128)
        relaid = (frames, slabs * rows, per, chans)
        parts = 4 if slabs * rows % 4 == 0 else 1
        relaid = call(
            unpack_kernel,
            "unpack",
            [(moved, HBM)],
            [(bf16(relaid), HBM)],
            [vmem16(moved.shape), vmem16(relaid), pltpu.SemaphoreType.DMA((parts,)), pltpu.SemaphoreType.DMA((parts,))],
        )
    else:
        relaid = lax.all_to_all(grad, "slab", split_axis=2, concat_axis=1, tiled=True)

    feat_v, kern_v, gain_v, shift_v, _ = lax.optimization_barrier((feat_v, kern_v, gain_v, shift_v, grad))
    decoded, part, lhs = call(
        forward_local_kernel,
        "forward_local",
        [(a, VMEM) for a in (feat_v, cache, kern_v, gain_v, shift_v, bias)],
        [(bf16((frames, rows, chans, cols)), HBM), (partial, VMEM), (weights, VMEM)],
        [
            vmem16((rows * block, (past + frames) * cols)),
            vmem16((3, chans, 2 * block)),
            vmem16((frames, max(rows - 2, 1), chans, cols)),
            pltpu.SemaphoreType.DMA((max(rows - 2, 1),)),
        ],
        flops=HINT,
    )
    decoded = call(
        forward_edge_kernel,
        "forward_edge",
        [(act_in, HBM), (act_across, HBM)] + [(a, VMEM) for a in (part, lhs, gain_v, shift_v)] + [(decoded, HBM)],
        [(bf16((frames, rows, chans, cols)), HBM)],
        [
            vmem16((past + frames, chans, cols)),
            vmem16((past + frames, chans, cols)),
            vmem16((2, block, (past + frames) * cols)),
            vmem16((frames, edge_rows, chans, cols)),
            pltpu.SemaphoreType.DMA((2,)),
            pltpu.SemaphoreType.DMA((edge_rows,)),
        ],
        aliases={6: 0},
        flops=HINT,
    )
    return (jnp.swapaxes(decoded, 2, 3), relaid)


def solution(mesh):
    rows = P(None, ("grp", "slab"), None, None)
    return jax.shard_map(
        body,
        mesh=mesh,
        in_specs=(rows, rows, rows, P(), P(), P(), P()),
        out_specs=(rows, P(None, "grp", "slab", None)),
        check_vma=False,
    )
```

```python
import functools

import jax
import jax.numpy as jnp
from jax import lax
from jax.experimental import pallas as pl
from jax.experimental.pallas import tpu as pltpu
from jax.sharding import PartitionSpec as P

EPS = 1e-06
HINT = 10**10


def column(vector, cols):
    return jnp.transpose(jnp.broadcast_to(vector, (cols, vector.shape[-1])))


def shifted_to(dst, row0, lanes, x, order):
    chans, cols = x.shape
    x32 = x.astype(jnp.float32)
    at = lax.broadcasted_iota(jnp.int32, x.shape, 1)
    for n, s in enumerate(order):
        if s == 0:
            seen = x
        elif s == 1:
            seen = jnp.where(at < cols - 1, pltpu.roll(x32, cols - 1, 1), 0.0)
        else:
            seen = jnp.where(at > 0, pltpu.roll(x32, 1, 1), 0.0)
        dst[row0 + n * chans : row0 + (n + 1) * chans, lanes : lanes + cols] = seen.astype(dst.dtype)


def normalized(x, gain, shift):
    values = x.astype(jnp.float32)
    mean = jnp.sum(values * values, axis=0, keepdims=True) * (1.0 / values.shape[0])
    scale = lax.rsqrt(mean + EPS)
    return values, scale, values * scale * gain + shift


def side_by_side(dst, taps):
    chans = taps[0].shape[0]
    for k in range(0, len(taps), 2):
        pair = taps[k : k + 2]
        dst[:, k * chans : (k + len(pair)) * chans] = pair[0] if len(pair) == 1 else jnp.concatenate(pair, axis=1)


def local_taps(r, rows):
    first = max(r - 1, 0)
    last = min(r + 1, rows - 1)
    return first - (r - 1), last - first + 1, first


def dot(a, b):
    return jnp.dot(a, b, preferred_element_type=jnp.float32)


def grad_sum(lhs_of, stack, lo, hi, frames, cols):
    acc = [None] * frames
    for f0 in range(0, frames, 2):
        for t in range(2, -1, -1):
            g0 = f0 + 2 - t
            count = min(2, frames - g0)
            if count <= 0:
                continue
            part = dot(lhs_of(t), stack[lo:hi, g0 * cols : (g0 + count) * cols])
            for n in range(count):
                piece = part[:, n * cols : (n + 1) * cols]
                acc[f0 + n] = piece if acc[f0 + n] is None else acc[f0 + n] + piece
    return acc


def finish(act_grad, feat, cot, gain, shift):
    values, scale, normed = normalized(feat, gain, shift)
    sig = 1.0 / (1.0 + jnp.exp(-normed))
    norm_grad = act_grad * sig * (1.0 + normed * (1.0 - sig)) * gain
    inner = jnp.sum(norm_grad * values, axis=0, keepdims=True) * (1.0 / values.shape[0])
    return cot.astype(jnp.float32) + scale * norm_grad - values * (scale * scale * scale * inner)


def put_row(out, r, grads, packed):
    frames = len(grads)
    if packed:
        dests = out.shape[0]
        cols = grads[0].shape[1]
        wide = [g[:128] for g in grads]
        for f in range(0, frames, 2):
            wide.append(jnp.concatenate([grads[f][128:], grads[f + 1][128:]], axis=0))
        tiles = [jnp.transpose(w).reshape(dests, cols // dests, 128) for w in wide]
        out[:, r] = jnp.concatenate(tiles, axis=1).astype(jnp.bfloat16)
    else:
        for f in range(frames):
            out[f, r] = jnp.transpose(grads[f]).astype(jnp.bfloat16)


def fetch(pairs, sems):
    copies = [pltpu.make_async_copy(s, d, sems.at[n]) for n, (s, d) in enumerate(pairs)]
    for c in copies:
        c.start()
    return copies


def rows_sent(rows):
    inner = jnp.where(lax.rem(lax.axis_index("slab"), 2) == 0, rows - 1, 0)
    return inner, rows - 1 - inner


def staging_kernel(cot, to_inner, to_outer, sems):
    inner, outer = rows_sent(cot.shape[1])
    for c in fetch([(cot.at[:, inner], to_inner), (cot.at[:, outer], to_outer)], sems):
        c.wait()


def backward_local_kernel(
    cot, feat, cache, kern, gain_in, shift_in,
    out, to_inner, to_outer, partial, weights,
    stack, tail, sent, edge_sems, out_sem, *, packed,
):
    frames, rows, chans, cols = cot.shape
    past = cache.shape[0]
    block = 3 * chans
    edges = list(zip(rows_sent(rows), (to_inner, to_outer)))
    written = fetch(
        [(feat.at[:, row], to.at[pl.ds(past, frames)]) for row, to in edges]
        + [(cache.at[:, row], to.at[pl.ds(0, past)]) for row, to in edges],
        edge_sems,
    )
    for p in range(rows):
        for f in range(frames):
            shifted_to(stack, p * block, f * cols, cot[f, p], (1, 0, -1))
    for t in range(3):
        taps = [kern[t, 2 - d, j] for d in range(3) for j in range(3)]
        side_by_side(weights.at[t], taps)
        side_by_side(tail.at[t], taps[3:])
    gain = column(gain_in[...], cols)
    shift = column(shift_in[...], cols)
    for r in list(range(1, rows - 1)) + sorted({0, rows - 1}):
        d0, n, first = local_taps(r, rows)

        def lhs_of(t):
            if d0 == 1:
                return tail[t, :, : n * block]
            return weights[t, :, : n * block]

        acc = grad_sum(lhs_of, stack, first * block, (first + n) * block, frames, cols)
        if n == 3:
            grads = [finish(acc[f], feat[f, r], cot[f, r], gain, shift) for f in range(frames)]
            put_row(sent, r - 1, grads, packed)
            written.append(pltpu.make_async_copy(sent.at[:, r - 1], out.at[:, r], out_sem.at[r - 1]))
            written[-1].start()
        else:
            for f in range(frames):
                partial[min(r, 1), f] = acc[f]
    for c in written:
        c.wait()


def backward_edge_kernel(
    cot, inner, outer, feat, partial, weights, gain_in, shift_in, before, out, stack, sent, out_sem, *, packed
):
    del before
    frames, rows, chans, cols = cot.shape
    block = 3 * chans
    slot = jnp.where(lax.rem(lax.axis_index("slab"), 2) == 0, 1, 0)
    for f in range(frames):
        shifted_to(stack.at[slot], 0, f * cols, inner[f], (1, 0, -1))
        shifted_to(stack.at[1 - slot], 0, f * cols, outer[f], (1, 0, -1))
    gain = column(gain_in[...], cols)
    shift = column(shift_in[...], cols)
    written = []
    for edge, r in enumerate(sorted({0, rows - 1})):
        acc = [partial[edge, f] for f in range(frames)]
        for d, there in ((0, r == 0), (2, r == rows - 1)):
            if there:
                more = grad_sum(
                    lambda t: weights[t, :, d * block : (d + 1) * block], stack.at[d // 2], 0, block, frames, cols
                )
                acc = [a + b for a, b in zip(acc, more)]
        grads = [finish(acc[f], feat[f, r], cot[f, r], gain, shift) for f in range(frames)]
        put_row(sent, edge, grads, packed)
        written.append(pltpu.make_async_copy(sent.at[:, edge], out.at[:, r], out_sem.at[edge]))
        written[-1].start()
    for c in written:
        c.wait()


def conv_sum(lhs_of, stack, lo, hi, frames, cols):
    acc = []
    for f0 in range(0, frames, 2):
        count = min(2, frames - f0)
        total = None
        for t in range(3):
            part = dot(lhs_of(t), stack[lo:hi, (f0 + t) * cols : (f0 + t + count) * cols])
            total = part if total is None else total + part
        acc += [total[:, n * cols : (n + 1) * cols] for n in range(count)]
    return acc


def activated(x, gain, shift):
    _, _, normed = normalized(x, gain, shift)
    return normed / (1.0 + jnp.exp(-normed))


def forward_local_kernel(
    feat, cache, kern, gain_in, shift_in, bias_in, out, partial, weights, stack, tail, ready, out_sem
):
    frames, rows, chans, cols = feat.shape
    past = cache.shape[0]
    block = 3 * chans
    gain = column(gain_in[...], cols)
    shift = column(shift_in[...], cols)
    bias = column(bias_in[...], cols)
    for t in range(3):
        whole = jnp.transpose(kern[t].reshape(3 * block, chans))
        weights[t] = whole
        tail[t] = whole[:, block:]
    for p in range(rows):
        for f in range(past):
            shifted_to(stack, p * block, f * cols, cache[f, p], (-1, 0, 1))
        for f in range(frames):
            act = activated(feat[f, p], gain, shift).astype(jnp.bfloat16)
            shifted_to(stack, p * block, (past + f) * cols, act, (-1, 0, 1))
    written = []
    for r in list(range(1, rows - 1)) + sorted({0, rows - 1}):
        d0, n, first = local_taps(r, rows)

        def lhs_of(t):
            if d0 == 1:
                return tail[t, :, : n * block]
            return weights[t, :, : n * block]

        acc = conv_sum(lhs_of, stack, first * block, (first + n) * block, frames, cols)
        decoded = [feat[f, r].astype(jnp.float32) + acc[f] + bias for f in range(frames)]
        if n == 3:
            for f in range(frames):
                ready[f, r - 1] = decoded[f].astype(jnp.bfloat16)
            written.append(pltpu.make_async_copy(ready.at[:, r - 1], out.at[:, r], out_sem.at[r - 1]))
            written[-1].start()
        else:
            for f in range(frames):
                partial[min(r, 1), f] = decoded[f]
    for c in written:
        c.wait()


def forward_edge_kernel(
    inner_hbm, outer_hbm, partial, weights, gain_in, shift_in, before, out, inner, outer, stack, ready, sems, out_sem
):
    del before
    rows = out.shape[1]
    frames, chans, cols = partial.shape[1:]
    past = inner.shape[0] - frames
    block = 3 * chans
    arriving = fetch([(inner_hbm, inner), (outer_hbm, outer)], sems)
    index = lax.axis_index("slab")
    slot = jnp.where(lax.rem(index, 2) == 0, 1, 0)
    inside = jnp.logical_and(index > 0, index < lax.axis_size("slab") - 1)
    gain = column(gain_in[...], cols)
    shift = column(shift_in[...], cols)
    for n, (side, to, held) in enumerate(((inner, slot, None), (outer, 1 - slot, inside))):
        arriving[n].wait()
        for f in range(past):
            shifted_to(stack.at[to], 0, f * cols, side[f], (-1, 0, 1))
        for f in range(past, past + frames):
            act = activated(side[f], gain, shift)
            if held is not None:
                act = jnp.where(held, act, 0.0)
            shifted_to(stack.at[to], 0, f * cols, act.astype(jnp.bfloat16), (-1, 0, 1))
    written = []
    for edge, r in enumerate(sorted({0, rows - 1})):
        acc = [partial[edge, f] for f in range(frames)]
        for d, there in ((0, r == 0), (2, r == rows - 1)):
            if there:
                more = conv_sum(
                    lambda t: weights[t, :, d * block : (d + 1) * block], stack.at[d // 2], 0, block, frames, cols
                )
                acc = [a + b for a, b in zip(acc, more)]
        for f in range(frames):
            ready[f, edge] = acc[f].astype(jnp.bfloat16)
        written.append(pltpu.make_async_copy(ready.at[:, edge], out.at[:, r], out_sem.at[edge]))
        written[-1].start()
    for c in written:
        c.wait()


def unpack_kernel(src_hbm, out_hbm, src, out, in_sem, out_sem):
    frames, lines = out.shape[:2]
    parts = in_sem.shape[0]
    step = lines // parts
    spans = [pl.ds(n * step, step) for n in range(parts)]
    arriving = fetch([(src_hbm.at[s], src.at[s]) for s in spans], in_sem)
    leaving = [pltpu.make_async_copy(out.at[:, s], out_hbm.at[:, s], out_sem.at[n]) for n, s in enumerate(spans)]
    for n, s in enumerate(spans):
        arriving[n].wait()
        for f in range(frames):
            out[f, s, :, :128] = src[s, f * 8 : (f + 1) * 8, :]
            low = (frames + f // 2) * 8
            rest = src[s, low : low + 8, :]
            out[f, s, :, 128:] = rest[:, :, :64] if f % 2 == 0 else rest[:, :, 64:]
        leaving[n].start()
    for c in leaving:
        c.wait()


VMEM = functools.partial(pl.BlockSpec, memory_space=pltpu.VMEM)
HBM = functools.partial(pl.BlockSpec, memory_space=pltpu.HBM)


def call(kernel, name, ins, outs, scratch=(), aliases=None, flops=None):
    result = pl.pallas_call(
        kernel,
        out_shape=[pltpu.HBM(o.shape, o.dtype) if where is HBM else o for o, where in outs],
        in_specs=[where() for _, where in ins],
        out_specs=[where() for _, where in outs],
        scratch_shapes=list(scratch),
        input_output_aliases=aliases or {},
        compiler_params=pltpu.CompilerParams(vmem_limit_bytes=24 * 1024 * 1024),
        cost_estimate=flops and pl.CostEstimate(flops=flops, transcendentals=0, bytes_accessed=0),
        name=name,
    )(*[pltpu.with_memory_space_constraint(a, pltpu.HBM) if where is HBM else a for a, where in ins])
    return result[0] if len(outs) == 1 else result


def body(features, time_cache, cotangent, kernel, norm_gain, norm_shift, conv_bias):
    frames, rows, cols, chans = features.shape
    past = time_cache.shape[0]
    slabs = lax.axis_size("slab")
    within = [(i, i ^ 1) for i in range(slabs)]
    across = [(i, i + 1) for i in range(1, slabs - 1, 2)] + [(i + 1, i) for i in range(1, slabs - 1, 2)]
    feat = jnp.swapaxes(features, 2, 3)
    cache = jnp.swapaxes(time_cache, 2, 3)
    cot = jnp.swapaxes(cotangent, 2, 3)
    gain = norm_gain.reshape(1, chans)
    shift = norm_shift.reshape(1, chans)
    bias = conv_bias.reshape(1, chans)
    block = 3 * chans
    edge_rows = min(rows, 2)
    per = cols // slabs
    packed = per % 8 == 0 and frames % 2 == 0 and chans == 192
    bf16 = functools.partial(jax.ShapeDtypeStruct, dtype=jnp.bfloat16)
    vmem16 = functools.partial(pltpu.VMEM, dtype=jnp.bfloat16)
    partial = jax.ShapeDtypeStruct((edge_rows, frames, chans, cols), jnp.float32)
    weights = bf16((3, chans, 3 * block))

    def sent(n):
        return (slabs, n, frames * per * chans // 128, 128) if packed else (frames, n, cols, chans)

    cot_in, cot_across = call(
        staging_kernel,
        "staging",
        [(cot, HBM)],
        [(bf16((frames, chans, cols)), VMEM)] * 2,
        [pltpu.SemaphoreType.DMA((2,))],
        flops=HINT,
    )
    cot_in = lax.ppermute(cot_in, "slab", within)
    cot_across = lax.ppermute(cot_across, "slab", across)
    grad, act_in, act_across, part, lhs = call(
        functools.partial(backward_local_kernel, packed=packed),
        "backward_local",
        [(a, VMEM) for a in (cot, feat, cache, kernel, gain, shift)],
        [(bf16(sent(rows)), HBM)]
        + [(bf16((past + frames, chans, cols)), HBM)] * 2
        + [(partial, VMEM), (weights, VMEM)],
        [
            vmem16((rows * block, frames * cols)),
            vmem16((3, chans, 2 * block)),
            vmem16(sent(max(rows - 2, 1))),
            pltpu.SemaphoreType.DMA((4,)),
            pltpu.SemaphoreType.DMA((max(rows - 2, 1),)),
        ],
    )
    act_in = lax.ppermute(act_in, "slab", within)
    act_across = lax.ppermute(act_across, "slab", across)
    grad = call(
        functools.partial(backward_edge_kernel, packed=packed),
        "backward_edge",
        [(a, VMEM) for a in (cot, cot_in, cot_across, feat, part, lhs, gain, shift)] + [(grad, HBM)],
        [(bf16(sent(rows)), HBM)],
        [vmem16((2, block, frames * cols)), vmem16(sent(edge_rows)), pltpu.SemaphoreType.DMA((edge_rows,))],
        aliases={8: 0},
    )

    if packed:
        moved = lax.all_to_all(grad, "slab", split_axis=0, concat_axis=0, tiled=True)
        moved = moved.reshape(slabs * rows, -1, 128)
        relaid = (frames, slabs * rows, per, chans)
        parts = 4 if slabs * rows % 4 == 0 else 1
        relaid = call(
            unpack_kernel,
            "unpack",
            [(moved, HBM)],
            [(bf16(relaid), HBM)],
            [vmem16(moved.shape), vmem16(relaid), pltpu.SemaphoreType.DMA((parts,)), pltpu.SemaphoreType.DMA((parts,))],
        )
    else:
        relaid = lax.all_to_all(grad, "slab", split_axis=2, concat_axis=1, tiled=True)

    feat_v, kern_v, gain_v, shift_v, _ = lax.optimization_barrier((feat, kernel, gain, shift, grad))
    decoded, part, lhs = call(
        forward_local_kernel,
        "forward_local",
        [(a, VMEM) for a in (feat_v, cache, kern_v, gain_v, shift_v, bias)],
        [(bf16((frames, rows, chans, cols)), HBM), (partial, VMEM), (weights, VMEM)],
        [
            vmem16((rows * block, (past + frames) * cols)),
            vmem16((3, chans, 2 * block)),
            vmem16((frames, max(rows - 2, 1), chans, cols)),
            pltpu.SemaphoreType.DMA((max(rows - 2, 1),)),
        ],
        flops=HINT,
    )
    decoded = call(
        forward_edge_kernel,
        "forward_edge",
        [(act_in, HBM), (act_across, HBM)] + [(a, VMEM) for a in (part, lhs, gain_v, shift_v)] + [(decoded, HBM)],
        [(bf16((frames, rows, chans, cols)), HBM)],
        [
            vmem16((past + frames, chans, cols)),
            vmem16((past + frames, chans, cols)),
            vmem16((2, block, (past + frames) * cols)),
            vmem16((frames, edge_rows, chans, cols)),
            pltpu.SemaphoreType.DMA((2,)),
            pltpu.SemaphoreType.DMA((edge_rows,)),
        ],
        aliases={6: 0},
        flops=HINT,
    )
    return (jnp.swapaxes(decoded, 2, 3), relaid)


def solution(mesh):
    rows = P(None, ("grp", "slab"), None, None)
    return jax.shard_map(
        body,
        mesh=mesh,
        in_specs=(rows, rows, rows, P(), P(), P(), P()),
        out_specs=(rows, P(None, "grp", "slab", None)),
        check_vma=False,
    )
```

```python
import functools

import jax
import jax.numpy as jnp
from jax import lax
from jax.experimental import pallas as pl
from jax.experimental.pallas import tpu as pltpu
from jax.sharding import PartitionSpec as P

EPS = 1e-06
HINT = 10**10


def column(vector, cols):
    return jnp.transpose(jnp.broadcast_to(vector, (cols, vector.shape[-1])))


def shifted_to(dst, row0, lanes, x, order):
    chans, cols = x.shape
    x32 = x.astype(jnp.float32)
    at = lax.broadcasted_iota(jnp.int32, x.shape, 1)
    for n, s in enumerate(order):
        if s == 0:
            seen = x
        elif s == 1:
            seen = jnp.where(at < cols - 1, pltpu.roll(x32, cols - 1, 1), 0.0)
        else:
            seen = jnp.where(at > 0, pltpu.roll(x32, 1, 1), 0.0)
        dst[row0 + n * chans : row0 + (n + 1) * chans, lanes : lanes + cols] = seen.astype(dst.dtype)


def normalized(x, gain, shift):
    values = x.astype(jnp.float32)
    mean = jnp.sum(values * values, axis=0, keepdims=True) * (1.0 / values.shape[0])
    scale = lax.rsqrt(mean + EPS)
    return values, scale, values * scale * gain + shift


def side_by_side(dst, taps):
    chans = taps[0].shape[0]
    for k in range(0, len(taps), 2):
        pair = taps[k : k + 2]
        dst[:, k * chans : (k + len(pair)) * chans] = pair[0] if len(pair) == 1 else jnp.concatenate(pair, axis=1)


def local_taps(r, rows):
    first = max(r - 1, 0)
    last = min(r + 1, rows - 1)
    return first - (r - 1), last - first + 1, first


def dot(a, b):
    return jnp.dot(a, b, preferred_element_type=jnp.float32)


def grad_sum(lhs, k0, k1, stack, lo, hi, frames, cols):
    chans = lhs.shape[0] // 3
    acc = [None] * frames
    for g0 in range(0, frames, 2):
        count = min(2, frames - g0)
        reach = min(3, g0 + count)
        part = dot(lhs[: reach * chans, k0:k1], stack[lo:hi, g0 * cols : (g0 + count) * cols])
        for back in range(reach):
            for n in range(count):
                f = g0 + n - back
                if f >= 0:
                    piece = part[back * chans : (back + 1) * chans, n * cols : (n + 1) * cols]
                    acc[f] = piece if acc[f] is None else acc[f] + piece
    return acc


def finish(act_grad, feat, cot, gain, shift):
    values, scale, normed = normalized(feat, gain, shift)
    sig = 1.0 / (1.0 + jnp.exp(-normed))
    norm_grad = act_grad * sig * (1.0 + normed * (1.0 - sig)) * gain
    inner = jnp.sum(norm_grad * values, axis=0, keepdims=True) * (1.0 / values.shape[0])
    return cot.astype(jnp.float32) + scale * norm_grad - values * (scale * scale * scale * inner)


def put_row(out, r, grads, packed):
    frames = len(grads)
    if packed:
        dests = out.shape[0]
        cols = grads[0].shape[1]
        wide = [g[:128] for g in grads]
        for f in range(0, frames, 2):
            wide.append(jnp.concatenate([grads[f][128:], grads[f + 1][128:]], axis=0))
        tiles = [jnp.transpose(w).reshape(dests, cols // dests, 128) for w in wide]
        out[:, r] = jnp.concatenate(tiles, axis=1).astype(jnp.bfloat16)
    else:
        for f in range(frames):
            out[f, r] = jnp.transpose(grads[f]).astype(jnp.bfloat16)


def fetch(pairs, sems):
    copies = [pltpu.make_async_copy(s, d, sems.at[n]) for n, (s, d) in enumerate(pairs)]
    for c in copies:
        c.start()
    return copies


def rows_sent(rows):
    inner = jnp.where(lax.rem(lax.axis_index("slab"), 2) == 0, rows - 1, 0)
    return inner, rows - 1 - inner


def staging_kernel(cot, to_inner, to_outer, sems):
    inner, outer = rows_sent(cot.shape[1])
    for c in fetch([(cot.at[:, inner], to_inner), (cot.at[:, outer], to_outer)], sems):
        c.wait()


def backward_local_kernel(
    cot, feat, cache, kern, gain_in, shift_in,
    middle, to_outer, partial, weights,
    stack, tail, edge_sems, *, packed,
):
    frames, rows, chans, cols = cot.shape
    past = cache.shape[0]
    block = 3 * chans
    _, outer = rows_sent(rows)
    written = fetch(
        [(feat.at[:, outer], to_outer.at[pl.ds(past, frames)]), (cache.at[:, outer], to_outer.at[pl.ds(0, past)])],
        edge_sems,
    )
    for p in range(rows):
        for f in range(frames):
            shifted_to(stack, p * block, f * cols, cot[f, p], (1, 0, -1))
    for t in range(3):
        taps = [kern[t, 2 - d, j] for d in range(3) for j in range(3)]
        rows_of_t = pl.ds((2 - t) * chans, chans)
        side_by_side(weights.at[rows_of_t], taps)
        side_by_side(tail.at[rows_of_t], taps[3:])
    gain = column(gain_in[...], cols)
    shift = column(shift_in[...], cols)
    for r in range(rows):
        d0, n, first = local_taps(r, rows)
        lhs = tail if d0 == 1 else weights
        acc = grad_sum(lhs, 0, n * block, stack, first * block, (first + n) * block, frames, cols)
        if n == 3:
            grads = [finish(acc[f], feat[f, r], cot[f, r], gain, shift) for f in range(frames)]
            put_row(middle, r - 1, grads, packed)
        else:
            for f in range(frames):
                partial[min(r, 1), f] = acc[f]
    for c in written:
        c.wait()


def backward_edge_kernel(
    cot, inner, outer, feat, partial, weights, gain_in, shift_in, middle, out, stack, sent, out_sem, *, packed
):
    frames, rows, chans, cols = cot.shape
    block = 3 * chans
    written = []
    if rows > 2:
        written.append(pltpu.make_async_copy(middle, out.at[:, 1 : rows - 1], out_sem.at[2]))
        written[0].start()
    slot = jnp.where(lax.rem(lax.axis_index("slab"), 2) == 0, 1, 0)
    for f in range(frames):
        shifted_to(stack.at[slot], 0, f * cols, inner[f], (1, 0, -1))
        shifted_to(stack.at[1 - slot], 0, f * cols, outer[f], (1, 0, -1))
    gain = column(gain_in[...], cols)
    shift = column(shift_in[...], cols)
    for edge, r in enumerate(sorted({0, rows - 1})):
        acc = [partial[edge, f] for f in range(frames)]
        for d, there in ((0, r == 0), (2, r == rows - 1)):
            if there:
                more = grad_sum(weights, d * block, (d + 1) * block, stack.at[d // 2], 0, block, frames, cols)
                acc = [a + b for a, b in zip(acc, more)]
        grads = [finish(acc[f], feat[f, r], cot[f, r], gain, shift) for f in range(frames)]
        put_row(sent, edge, grads, packed)
        written.append(pltpu.make_async_copy(sent.at[:, edge], out.at[:, r], out_sem.at[edge]))
        written[-1].start()
    for c in written:
        c.wait()


def conv_sum(lhs_of, stack, lo, hi, frames, cols):
    acc = []
    for f0 in range(0, frames, 2):
        count = min(2, frames - f0)
        total = None
        for t in range(3):
            part = dot(lhs_of(t), stack[lo:hi, (f0 + t) * cols : (f0 + t + count) * cols])
            total = part if total is None else total + part
        acc += [total[:, n * cols : (n + 1) * cols] for n in range(count)]
    return acc


def activated(x, gain, shift):
    _, _, normed = normalized(x, gain, shift)
    return normed / (1.0 + jnp.exp(-normed))


def forward_local_kernel(
    feat, cache, kern, gain_in, shift_in, bias_in,
    out, to_inner, partial, weights, stack, tail, ready, out_sem, edge_sems,
):
    frames, rows, chans, cols = feat.shape
    past = cache.shape[0]
    block = 3 * chans
    gain = column(gain_in[...], cols)
    shift = column(shift_in[...], cols)
    bias = column(bias_in[...], cols)
    inner, _ = rows_sent(rows)
    written = fetch(
        [(feat.at[:, inner], to_inner.at[pl.ds(past, frames)]), (cache.at[:, inner], to_inner.at[pl.ds(0, past)])],
        edge_sems,
    )
    for t in range(3):
        whole = jnp.transpose(kern[t].reshape(3 * block, chans))
        weights[t] = whole
        tail[t] = whole[:, block:]
    for p in range(rows):
        for f in range(past):
            shifted_to(stack, p * block, f * cols, cache[f, p], (-1, 0, 1))
        for f in range(frames):
            act = activated(feat[f, p], gain, shift).astype(jnp.bfloat16)
            shifted_to(stack, p * block, (past + f) * cols, act, (-1, 0, 1))
    for r in list(range(1, rows - 1)) + sorted({0, rows - 1}):
        d0, n, first = local_taps(r, rows)

        def lhs_of(t):
            if d0 == 1:
                return tail[t, :, : n * block]
            return weights[t, :, : n * block]

        acc = conv_sum(lhs_of, stack, first * block, (first + n) * block, frames, cols)
        decoded = [feat[f, r].astype(jnp.float32) + acc[f] + bias for f in range(frames)]
        if n == 3:
            for f in range(frames):
                ready[f, r - 1] = decoded[f].astype(jnp.bfloat16)
            written.append(pltpu.make_async_copy(ready.at[:, r - 1], out.at[:, r], out_sem.at[r - 1]))
            written[-1].start()
        else:
            for f in range(frames):
                partial[min(r, 1), f] = decoded[f]
    for c in written:
        c.wait()


def forward_edge_kernel(
    inner_hbm, outer_hbm, partial, weights, gain_in, shift_in, before, out, inner, outer, stack, ready, sems, out_sem
):
    del before
    rows = out.shape[1]
    frames, chans, cols = partial.shape[1:]
    past = inner.shape[0] - frames
    block = 3 * chans
    arriving = fetch([(inner_hbm, inner), (outer_hbm, outer)], sems)
    index = lax.axis_index("slab")
    slot = jnp.where(lax.rem(index, 2) == 0, 1, 0)
    inside = jnp.logical_and(index > 0, index < lax.axis_size("slab") - 1)
    gain = column(gain_in[...], cols)
    shift = column(shift_in[...], cols)
    for n, (side, to, held) in enumerate(((inner, slot, None), (outer, 1 - slot, inside))):
        arriving[n].wait()
        for f in range(past):
            shifted_to(stack.at[to], 0, f * cols, side[f], (-1, 0, 1))
        for f in range(past, past + frames):
            act = activated(side[f], gain, shift)
            if held is not None:
                act = jnp.where(held, act, 0.0)
            shifted_to(stack.at[to], 0, f * cols, act.astype(jnp.bfloat16), (-1, 0, 1))
    written = []
    for edge, r in enumerate(sorted({0, rows - 1})):
        acc = [partial[edge, f] for f in range(frames)]
        for d, there in ((0, r == 0), (2, r == rows - 1)):
            if there:
                more = conv_sum(
                    lambda t: weights[t, :, d * block : (d + 1) * block], stack.at[d // 2], 0, block, frames, cols
                )
                acc = [a + b for a, b in zip(acc, more)]
        for f in range(frames):
            ready[f, edge] = acc[f].astype(jnp.bfloat16)
        written.append(pltpu.make_async_copy(ready.at[:, edge], out.at[:, r], out_sem.at[edge]))
        written[-1].start()
    for c in written:
        c.wait()


def unpack_kernel(src_hbm, out_hbm, src, out, in_sem, out_sem):
    frames, lines = out.shape[:2]
    parts = in_sem.shape[0]
    step = lines // parts
    spans = [pl.ds(n * step, step) for n in range(parts)]
    arriving = fetch([(src_hbm.at[s], src.at[s]) for s in spans], in_sem)
    leaving = [pltpu.make_async_copy(out.at[:, s], out_hbm.at[:, s], out_sem.at[n]) for n, s in enumerate(spans)]
    for n, s in enumerate(spans):
        arriving[n].wait()
        for f in range(frames):
            out[f, s, :, :128] = src[s, f * 8 : (f + 1) * 8, :]
            low = (frames + f // 2) * 8
            rest = src[s, low : low + 8, :]
            out[f, s, :, 128:] = rest[:, :, :64] if f % 2 == 0 else rest[:, :, 64:]
        leaving[n].start()
    for c in leaving:
        c.wait()


VMEM = functools.partial(pl.BlockSpec, memory_space=pltpu.VMEM)
HBM = functools.partial(pl.BlockSpec, memory_space=pltpu.HBM)


def call(kernel, name, ins, outs, scratch=(), aliases=None, flops=None):
    result = pl.pallas_call(
        kernel,
        out_shape=[pltpu.HBM(o.shape, o.dtype) if where is HBM else o for o, where in outs],
        in_specs=[where() for _, where in ins],
        out_specs=[where() for _, where in outs],
        scratch_shapes=list(scratch),
        input_output_aliases=aliases or {},
        compiler_params=pltpu.CompilerParams(vmem_limit_bytes=24 * 1024 * 1024),
        cost_estimate=flops and pl.CostEstimate(flops=flops, transcendentals=0, bytes_accessed=0),
        name=name,
    )(*[pltpu.with_memory_space_constraint(a, pltpu.HBM) if where is HBM else a for a, where in ins])
    return result[0] if len(outs) == 1 else result


def body(features, time_cache, cotangent, kernel, norm_gain, norm_shift, conv_bias):
    frames, rows, cols, chans = features.shape
    past = time_cache.shape[0]
    slabs = lax.axis_size("slab")
    within = [(i, i ^ 1) for i in range(slabs)]
    across = [(i, i + 1) for i in range(1, slabs - 1, 2)] + [(i + 1, i) for i in range(1, slabs - 1, 2)]
    feat = jnp.swapaxes(features, 2, 3)
    cache = jnp.swapaxes(time_cache, 2, 3)
    cot = jnp.swapaxes(cotangent, 2, 3)
    gain = norm_gain.reshape(1, chans)
    shift = norm_shift.reshape(1, chans)
    bias = conv_bias.reshape(1, chans)
    block = 3 * chans
    edge_rows = min(rows, 2)
    per = cols // slabs
    packed = per % 8 == 0 and frames % 2 == 0 and chans == 192
    bf16 = functools.partial(jax.ShapeDtypeStruct, dtype=jnp.bfloat16)
    vmem16 = functools.partial(pltpu.VMEM, dtype=jnp.bfloat16)
    partial = jax.ShapeDtypeStruct((edge_rows, frames, chans, cols), jnp.float32)
    weights = bf16((3, chans, 3 * block))

    def sent(n):
        return (slabs, n, frames * per * chans // 128, 128) if packed else (frames, n, cols, chans)

    cot_in, cot_across = call(
        staging_kernel,
        "staging",
        [(cot, HBM)],
        [(bf16((frames, chans, cols)), VMEM)] * 2,
        [pltpu.SemaphoreType.DMA((2,))],
        flops=HINT,
    )
    cot_in = lax.ppermute(cot_in, "slab", within)
    cot_across = lax.ppermute(cot_across, "slab", across)
    middle, act_across, part, lhs = call(
        functools.partial(backward_local_kernel, packed=packed),
        "backward_local",
        [(a, VMEM) for a in (cot, feat, cache, kernel, gain, shift)],
        [(bf16(sent(max(rows - 2, 1))), VMEM)]
        + [(bf16((past + frames, chans, cols)), HBM)]
        + [(partial, VMEM), (bf16((3 * chans, 3 * block)), VMEM)],
        [
            vmem16((rows * block, frames * cols)),
            vmem16((3 * chans, 2 * block)),
            pltpu.SemaphoreType.DMA((2,)),
        ],
    )
    act_across = lax.ppermute(act_across, "slab", across)
    grad = call(
        functools.partial(backward_edge_kernel, packed=packed),
        "backward_edge",
        [(a, VMEM) for a in (cot, cot_in, cot_across, feat, part, lhs, gain, shift, middle)],
        [(bf16(sent(rows)), HBM)],
        [vmem16((2, block, frames * cols)), vmem16(sent(edge_rows)), pltpu.SemaphoreType.DMA((3,))],
    )

    if packed:
        moved = lax.all_to_all(grad, "slab", split_axis=0, concat_axis=0, tiled=True)
        moved = moved.reshape(slabs * rows, -1, 128)
        relaid = (frames, slabs * rows, per, chans)
        parts = 4 if slabs * rows % 4 == 0 else 1
        relaid = call(
            unpack_kernel,
            "unpack",
            [(moved, HBM)],
            [(bf16(relaid), HBM)],
            [vmem16(moved.shape), vmem16(relaid), pltpu.SemaphoreType.DMA((parts,)), pltpu.SemaphoreType.DMA((parts,))],
        )
    else:
        relaid = lax.all_to_all(grad, "slab", split_axis=2, concat_axis=1, tiled=True)

    feat_v, kern_v, gain_v, shift_v, _ = lax.optimization_barrier((feat, kernel, gain, shift, grad))
    decoded, act_in, part, lhs = call(
        forward_local_kernel,
        "forward_local",
        [(a, VMEM) for a in (feat_v, cache, kern_v, gain_v, shift_v, bias)],
        [(bf16((frames, rows, chans, cols)), HBM), (bf16((past + frames, chans, cols)), HBM), (partial, VMEM), (weights, VMEM)],
        [
            vmem16((rows * block, (past + frames) * cols)),
            vmem16((3, chans, 2 * block)),
            vmem16((frames, max(rows - 2, 1), chans, cols)),
            pltpu.SemaphoreType.DMA((max(rows - 2, 1),)),
            pltpu.SemaphoreType.DMA((2,)),
        ],
        flops=HINT,
    )
    act_in = lax.ppermute(act_in, "slab", within)
    decoded = call(
        forward_edge_kernel,
        "forward_edge",
        [(act_in, HBM), (act_across, HBM)] + [(a, VMEM) for a in (part, lhs, gain_v, shift_v)] + [(decoded, HBM)],
        [(bf16((frames, rows, chans, cols)), HBM)],
        [
            vmem16((past + frames, chans, cols)),
            vmem16((past + frames, chans, cols)),
            vmem16((2, block, (past + frames) * cols)),
            vmem16((frames, edge_rows, chans, cols)),
            pltpu.SemaphoreType.DMA((2,)),
            pltpu.SemaphoreType.DMA((edge_rows,)),
        ],
        aliases={6: 0},
    )
    return (jnp.swapaxes(decoded, 2, 3), relaid)


def solution(mesh):
    rows = P(None, ("grp", "slab"), None, None)
    return jax.shard_map(
        body,
        mesh=mesh,
        in_specs=(rows, rows, rows, P(), P(), P(), P()),
        out_specs=(rows, P(None, "grp", "slab", None)),
        check_vma=False,
    )
```

```python
import functools

import jax
import jax.numpy as jnp
from jax import lax
from jax.experimental import pallas as pl
from jax.experimental.pallas import tpu as pltpu
from jax.sharding import PartitionSpec as P

EPS = 1e-06
HINT = 10**10


def column(vector, cols):
    return jnp.transpose(jnp.broadcast_to(vector, (cols, vector.shape[-1])))


def shifted_to(dst, row0, lanes, x, order):
    chans, cols = x.shape
    x32 = x.astype(jnp.float32)
    at = lax.broadcasted_iota(jnp.int32, x.shape, 1)
    for n, s in enumerate(order):
        if s == 0:
            seen = x
        elif s == 1:
            seen = jnp.where(at < cols - 1, pltpu.roll(x32, cols - 1, 1), 0.0)
        else:
            seen = jnp.where(at > 0, pltpu.roll(x32, 1, 1), 0.0)
        dst[pl.ds(row0 + n * chans, chans), pl.ds(lanes, cols)] = seen.astype(dst.dtype)


def normalized(x, gain, shift):
    values = x.astype(jnp.float32)
    mean = jnp.sum(values * values, axis=0, keepdims=True) * (1.0 / values.shape[0])
    scale = lax.rsqrt(mean + EPS)
    return values, scale, values * scale * gain + shift


def side_by_side(dst, taps):
    chans = taps[0].shape[0]
    for k in range(0, len(taps), 2):
        pair = taps[k : k + 2]
        dst[:, k * chans : (k + len(pair)) * chans] = pair[0] if len(pair) == 1 else jnp.concatenate(pair, axis=1)


def local_taps(r, rows):
    first = max(r - 1, 0)
    last = min(r + 1, rows - 1)
    return first - (r - 1), last - first + 1, first


def dot(a, b):
    return jnp.dot(a, b, preferred_element_type=jnp.float32)


def grad_sum(lhs, k0, k1, stack, lo, hi, frames, cols):
    chans = lhs.shape[0] // 3
    acc = [None] * frames
    for g0 in range(0, frames, 2):
        count = min(2, frames - g0)
        reach = min(3, g0 + count)
        part = dot(lhs[: reach * chans, k0:k1], stack[lo:hi, g0 * cols : (g0 + count) * cols])
        for back in range(reach):
            for n in range(count):
                f = g0 + n - back
                if f >= 0:
                    piece = part[back * chans : (back + 1) * chans, n * cols : (n + 1) * cols]
                    acc[f] = piece if acc[f] is None else acc[f] + piece
    return acc


def finish(act_grad, feat, cot, gain, shift):
    values, scale, normed = normalized(feat, gain, shift)
    sig = 1.0 / (1.0 + jnp.exp(-normed))
    norm_grad = act_grad * sig * (1.0 + normed * (1.0 - sig)) * gain
    inner = jnp.sum(norm_grad * values, axis=0, keepdims=True) * (1.0 / values.shape[0])
    return cot.astype(jnp.float32) + scale * norm_grad - values * (scale * scale * scale * inner)


def put_row(out, r, grads, packed):
    frames = len(grads)
    if packed:
        dests = out.shape[0]
        cols = grads[0].shape[1]
        wide = [g[:128] for g in grads]
        for f in range(0, frames, 2):
            wide.append(jnp.concatenate([grads[f][128:], grads[f + 1][128:]], axis=0))
        tiles = [jnp.transpose(w).reshape(dests, cols // dests, 128) for w in wide]
        out[:, r] = jnp.concatenate(tiles, axis=1).astype(jnp.bfloat16)
    else:
        for f in range(frames):
            out[f, r] = jnp.transpose(grads[f]).astype(jnp.bfloat16)


def fetch(pairs, sems):
    copies = [pltpu.make_async_copy(s, d, sems.at[n]) for n, (s, d) in enumerate(pairs)]
    for c in copies:
        c.start()
    return copies


def rows_sent(rows):
    inner = jnp.where(lax.rem(lax.axis_index("slab"), 2) == 0, rows - 1, 0)
    return inner, rows - 1 - inner


def staging_kernel(cot, to_outer, to_inner, sems):
    inner, outer = rows_sent(cot.shape[1])
    for c in fetch([(cot.at[:, inner], to_inner), (cot.at[:, outer], to_outer)], sems):
        c.wait()


def backward_local_kernel(
    cot, feat, cache, kern, gain_in, shift_in,
    middle, to_outer, partial, weights,
    stack, tail, edge_sems, *, packed,
):
    frames, rows, chans, cols = cot.shape
    past = cache.shape[0]
    block = 3 * chans
    _, outer = rows_sent(rows)
    written = fetch(
        [(feat.at[:, outer], to_outer.at[pl.ds(past, frames)]), (cache.at[:, outer], to_outer.at[pl.ds(0, past)])],
        edge_sems,
    )
    @pl.loop(0, rows)
    def _(p):
        for f in range(frames):
            shifted_to(stack, pl.multiple_of(p * block, 64), f * cols, cot[f, p], (1, 0, -1))

    for t in range(3):
        taps = [kern[t, 2 - d, j] for d in range(3) for j in range(3)]
        rows_of_t = pl.ds((2 - t) * chans, chans)
        side_by_side(weights.at[rows_of_t], taps)
        side_by_side(tail.at[rows_of_t], taps[3:])
    gain = column(gain_in[...], cols)
    shift = column(shift_in[...], cols)
    for r in range(rows):
        d0, n, first = local_taps(r, rows)
        lhs = tail if d0 == 1 else weights
        acc = grad_sum(lhs, 0, n * block, stack, first * block, (first + n) * block, frames, cols)
        if n == 3:
            grads = [finish(acc[f], feat[f, r], cot[f, r], gain, shift) for f in range(frames)]
            put_row(middle, r - 1, grads, packed)
        else:
            for f in range(frames):
                partial[min(r, 1), f] = acc[f]
    for c in written:
        c.wait()


def backward_edge_kernel(
    cot, outer, inner, feat, partial, weights, gain_in, shift_in, middle, out, stack, sent, out_sem, *, packed
):
    frames, rows, chans, cols = cot.shape
    block = 3 * chans
    written = []
    if rows > 2:
        written.append(pltpu.make_async_copy(middle, out.at[:, 1 : rows - 1], out_sem.at[2]))
        written[0].start()
    slot = jnp.where(lax.rem(lax.axis_index("slab"), 2) == 0, 1, 0)
    for f in range(frames):
        shifted_to(stack.at[slot], 0, f * cols, inner[f], (1, 0, -1))
        shifted_to(stack.at[1 - slot], 0, f * cols, outer[f], (1, 0, -1))
    gain = column(gain_in[...], cols)
    shift = column(shift_in[...], cols)
    for edge, r in enumerate(sorted({0, rows - 1})):
        acc = [partial[edge, f] for f in range(frames)]
        for d, there in ((0, r == 0), (2, r == rows - 1)):
            if there:
                more = grad_sum(weights, d * block, (d + 1) * block, stack.at[d // 2], 0, block, frames, cols)
                acc = [a + b for a, b in zip(acc, more)]
        grads = [finish(acc[f], feat[f, r], cot[f, r], gain, shift) for f in range(frames)]
        put_row(sent, edge, grads, packed)
        written.append(pltpu.make_async_copy(sent.at[:, edge], out.at[:, r], out_sem.at[edge]))
        written[-1].start()
    for c in written:
        c.wait()


def conv_sum(lhs_of, stack, lo, hi, frames, cols):
    acc = []
    for f0 in range(0, frames, 2):
        count = min(2, frames - f0)
        total = None
        for t in range(3):
            part = dot(lhs_of(t), stack[lo:hi, (f0 + t) * cols : (f0 + t + count) * cols])
            total = part if total is None else total + part
        acc += [total[:, n * cols : (n + 1) * cols] for n in range(count)]
    return acc


def activated(x, gain, shift):
    _, _, normed = normalized(x, gain, shift)
    return normed / (1.0 + jnp.exp(-normed))


def forward_local_kernel(
    feat, cache, kern, gain_in, shift_in, bias_in,
    out, to_inner, partial, weights, stack, tail, ready, out_sem, edge_sems,
):
    frames, rows, chans, cols = feat.shape
    past = cache.shape[0]
    block = 3 * chans
    gain = column(gain_in[...], cols)
    shift = column(shift_in[...], cols)
    bias = column(bias_in[...], cols)
    inner, _ = rows_sent(rows)
    written = fetch(
        [(feat.at[:, inner], to_inner.at[pl.ds(past, frames)]), (cache.at[:, inner], to_inner.at[pl.ds(0, past)])],
        edge_sems,
    )
    for t in range(3):
        whole = jnp.transpose(kern[t].reshape(3 * block, chans))
        weights[t] = whole
        tail[t] = whole[:, block:]
    for p in range(rows):
        for f in range(past):
            shifted_to(stack, p * block, f * cols, cache[f, p], (-1, 0, 1))
        for f in range(frames):
            act = activated(feat[f, p], gain, shift).astype(jnp.bfloat16)
            shifted_to(stack, p * block, (past + f) * cols, act, (-1, 0, 1))
    for r in list(range(1, rows - 1)) + sorted({0, rows - 1}):
        d0, n, first = local_taps(r, rows)

        def lhs_of(t):
            if d0 == 1:
                return tail[t, :, : n * block]
            return weights[t, :, : n * block]

        acc = conv_sum(lhs_of, stack, first * block, (first + n) * block, frames, cols)
        decoded = [feat[f, r].astype(jnp.float32) + acc[f] + bias for f in range(frames)]
        if n == 3:
            for f in range(frames):
                ready[f, r - 1] = decoded[f].astype(jnp.bfloat16)
            written.append(pltpu.make_async_copy(ready.at[:, r - 1], out.at[:, r], out_sem.at[r - 1]))
            written[-1].start()
        else:
            for f in range(frames):
                partial[min(r, 1), f] = decoded[f]
    for c in written:
        c.wait()


def forward_edge_kernel(
    inner_hbm, outer_hbm, partial, weights, gain_in, shift_in, before, out, inner, outer, stack, ready, sems, out_sem
):
    del before
    rows = out.shape[1]
    frames, chans, cols = partial.shape[1:]
    past = inner.shape[0] - frames
    block = 3 * chans
    arriving = fetch([(inner_hbm, inner), (outer_hbm, outer)], sems)
    index = lax.axis_index("slab")
    slot = jnp.where(lax.rem(index, 2) == 0, 1, 0)
    inside = jnp.logical_and(index > 0, index < lax.axis_size("slab") - 1)
    gain = column(gain_in[...], cols)
    shift = column(shift_in[...], cols)
    for n, (side, to, held) in enumerate(((inner, slot, None), (outer, 1 - slot, inside))):
        arriving[n].wait()
        for f in range(past):
            shifted_to(stack.at[to], 0, f * cols, side[f], (-1, 0, 1))
        for f in range(past, past + frames):
            act = activated(side[f], gain, shift)
            if held is not None:
                act = jnp.where(held, act, 0.0)
            shifted_to(stack.at[to], 0, f * cols, act.astype(jnp.bfloat16), (-1, 0, 1))
    written = []
    for edge, r in enumerate(sorted({0, rows - 1})):
        acc = [partial[edge, f] for f in range(frames)]
        for d, there in ((0, r == 0), (2, r == rows - 1)):
            if there:
                more = conv_sum(
                    lambda t: weights[t, :, d * block : (d + 1) * block], stack.at[d // 2], 0, block, frames, cols
                )
                acc = [a + b for a, b in zip(acc, more)]
        for f in range(frames):
            ready[f, edge] = acc[f].astype(jnp.bfloat16)
        written.append(pltpu.make_async_copy(ready.at[:, edge], out.at[:, r], out_sem.at[edge]))
        written[-1].start()
    for c in written:
        c.wait()


def unpack_kernel(src_hbm, out_hbm, src, out, in_sem, out_sem):
    frames, lines = out.shape[:2]
    parts = in_sem.shape[0]
    step = lines // parts
    spans = [pl.ds(n * step, step) for n in range(parts)]
    arriving = fetch([(src_hbm.at[s], src.at[s]) for s in spans], in_sem)
    leaving = [pltpu.make_async_copy(out.at[:, s], out_hbm.at[:, s], out_sem.at[n]) for n, s in enumerate(spans)]
    for n, s in enumerate(spans):
        arriving[n].wait()
        for f in range(frames):
            out[f, s, :, :128] = src[s, f * 8 : (f + 1) * 8, :]
            low = (frames + f // 2) * 8
            rest = src[s, low : low + 8, :]
            out[f, s, :, 128:] = rest[:, :, :64] if f % 2 == 0 else rest[:, :, 64:]
        leaving[n].start()
    for c in leaving:
        c.wait()


VMEM = functools.partial(pl.BlockSpec, memory_space=pltpu.VMEM)
HBM = functools.partial(pl.BlockSpec, memory_space=pltpu.HBM)


def call(kernel, name, ins, outs, scratch=(), aliases=None, flops=None):
    result = pl.pallas_call(
        kernel,
        out_shape=[pltpu.HBM(o.shape, o.dtype) if where is HBM else o for o, where in outs],
        in_specs=[where() for _, where in ins],
        out_specs=[where() for _, where in outs],
        scratch_shapes=list(scratch),
        input_output_aliases=aliases or {},
        compiler_params=pltpu.CompilerParams(vmem_limit_bytes=24 * 1024 * 1024),
        cost_estimate=flops and pl.CostEstimate(flops=flops, transcendentals=0, bytes_accessed=0),
        name=name,
    )(*[pltpu.with_memory_space_constraint(a, pltpu.HBM) if where is HBM else a for a, where in ins])
    return result[0] if len(outs) == 1 else result


def body(features, time_cache, cotangent, kernel, norm_gain, norm_shift, conv_bias):
    frames, rows, cols, chans = features.shape
    past = time_cache.shape[0]
    slabs = lax.axis_size("slab")
    within = [(i, i ^ 1) for i in range(slabs)]
    across = [(i, i + 1) for i in range(1, slabs - 1, 2)] + [(i + 1, i) for i in range(1, slabs - 1, 2)]
    feat = jnp.swapaxes(features, 2, 3)
    cache = jnp.swapaxes(time_cache, 2, 3)
    cot = jnp.swapaxes(cotangent, 2, 3)
    gain = norm_gain.reshape(1, chans)
    shift = norm_shift.reshape(1, chans)
    bias = conv_bias.reshape(1, chans)
    block = 3 * chans
    edge_rows = min(rows, 2)
    per = cols // slabs
    packed = per % 8 == 0 and frames % 2 == 0 and chans == 192
    bf16 = functools.partial(jax.ShapeDtypeStruct, dtype=jnp.bfloat16)
    vmem16 = functools.partial(pltpu.VMEM, dtype=jnp.bfloat16)
    partial = jax.ShapeDtypeStruct((edge_rows, frames, chans, cols), jnp.float32)
    weights = bf16((3, chans, 3 * block))

    def sent(n):
        return (slabs, n, frames * per * chans // 128, 128) if packed else (frames, n, cols, chans)

    cot_across, cot_in = call(
        staging_kernel,
        "staging",
        [(cot, HBM)],
        [(bf16((frames, chans, cols)), VMEM)] * 2,
        [pltpu.SemaphoreType.DMA((2,))],
        flops=HINT,
    )
    cot_across = lax.ppermute(cot_across, "slab", across)
    cot_in = lax.ppermute(cot_in, "slab", within)
    middle, act_across, part, lhs = call(
        functools.partial(backward_local_kernel, packed=packed),
        "backward_local",
        [(a, VMEM) for a in (cot, feat, cache, kernel, gain, shift)],
        [(bf16(sent(max(rows - 2, 1))), VMEM)]
        + [(bf16((past + frames, chans, cols)), HBM)]
        + [(partial, VMEM), (bf16((3 * chans, 3 * block)), VMEM)],
        [
            vmem16((rows * block, frames * cols)),
            vmem16((3 * chans, 2 * block)),
            pltpu.SemaphoreType.DMA((2,)),
        ],
    )
    act_across = lax.ppermute(act_across, "slab", across)
    grad = call(
        functools.partial(backward_edge_kernel, packed=packed),
        "backward_edge",
        [(a, VMEM) for a in (cot, cot_across, cot_in, feat, part, lhs, gain, shift, middle)],
        [(bf16(sent(rows)), HBM)],
        [vmem16((2, block, frames * cols)), vmem16(sent(edge_rows)), pltpu.SemaphoreType.DMA((3,))],
    )

    if packed:
        moved = lax.all_to_all(grad, "slab", split_axis=0, concat_axis=0, tiled=True)
        moved = moved.reshape(slabs * rows, -1, 128)
        relaid = (frames, slabs * rows, per, chans)
        parts = 4 if slabs * rows % 4 == 0 else 1
        relaid = call(
            unpack_kernel,
            "unpack",
            [(moved, HBM)],
            [(bf16(relaid), HBM)],
            [vmem16(moved.shape), vmem16(relaid), pltpu.SemaphoreType.DMA((parts,)), pltpu.SemaphoreType.DMA((parts,))],
        )
    else:
        relaid = lax.all_to_all(grad, "slab", split_axis=2, concat_axis=1, tiled=True)

    feat_v, kern_v, gain_v, shift_v, _ = lax.optimization_barrier((feat, kernel, gain, shift, grad))
    decoded, act_in, part, lhs = call(
        forward_local_kernel,
        "forward_local",
        [(a, VMEM) for a in (feat_v, cache, kern_v, gain_v, shift_v, bias)],
        [(bf16((frames, rows, chans, cols)), HBM), (bf16((past + frames, chans, cols)), HBM), (partial, VMEM), (weights, VMEM)],
        [
            vmem16((rows * block, (past + frames) * cols)),
            vmem16((3, chans, 2 * block)),
            vmem16((frames, max(rows - 2, 1), chans, cols)),
            pltpu.SemaphoreType.DMA((max(rows - 2, 1),)),
            pltpu.SemaphoreType.DMA((2,)),
        ],
        flops=HINT,
    )
    act_in = lax.ppermute(act_in, "slab", within)
    decoded = call(
        forward_edge_kernel,
        "forward_edge",
        [(act_in, HBM), (act_across, HBM)] + [(a, VMEM) for a in (part, lhs, gain_v, shift_v)] + [(decoded, HBM)],
        [(bf16((frames, rows, chans, cols)), HBM)],
        [
            vmem16((past + frames, chans, cols)),
            vmem16((past + frames, chans, cols)),
            vmem16((2, block, (past + frames) * cols)),
            vmem16((frames, edge_rows, chans, cols)),
            pltpu.SemaphoreType.DMA((2,)),
            pltpu.SemaphoreType.DMA((edge_rows,)),
        ],
        aliases={6: 0},
    )
    return (jnp.swapaxes(decoded, 2, 3), relaid)


def solution(mesh):
    rows = P(None, ("grp", "slab"), None, None)
    return jax.shard_map(
        body,
        mesh=mesh,
        in_specs=(rows, rows, rows, P(), P(), P(), P()),
        out_specs=(rows, P(None, "grp", "slab", None)),
        check_vma=False,
    )
```

```python
import functools

import jax
import jax.numpy as jnp
from jax import lax
from jax.experimental import pallas as pl
from jax.experimental.pallas import tpu as pltpu
from jax.sharding import PartitionSpec as P

EPS = 1e-06
HINT = 10**10


def column(vector, cols):
    return jnp.transpose(jnp.broadcast_to(vector, (cols, vector.shape[-1])))


def shifted_to(dst, row0, lanes, x, order):
    chans, cols = x.shape
    x32 = x.astype(jnp.float32)
    at = lax.broadcasted_iota(jnp.int32, x.shape, 1)
    for n, s in enumerate(order):
        if s == 0:
            seen = x
        elif s == 1:
            seen = jnp.where(at < cols - 1, pltpu.roll(x32, cols - 1, 1), 0.0)
        else:
            seen = jnp.where(at > 0, pltpu.roll(x32, 1, 1), 0.0)
        dst[pl.ds(row0 + n * chans, chans), pl.ds(lanes, cols)] = seen.astype(dst.dtype)


def normalized(x, gain, shift):
    values = x.astype(jnp.float32)
    mean = jnp.sum(values * values, axis=0, keepdims=True) * (1.0 / values.shape[0])
    scale = lax.rsqrt(mean + EPS)
    return values, scale, values * scale * gain + shift


def side_by_side(dst, taps):
    chans = taps[0].shape[0]
    for k in range(0, len(taps), 2):
        pair = taps[k : k + 2]
        dst[:, k * chans : (k + len(pair)) * chans] = pair[0] if len(pair) == 1 else jnp.concatenate(pair, axis=1)


def local_taps(r, rows):
    first = max(r - 1, 0)
    last = min(r + 1, rows - 1)
    return first - (r - 1), last - first + 1, first


def dot(a, b):
    return jnp.dot(a, b, preferred_element_type=jnp.float32)


def grad_sum(lhs, k0, k1, stack, lo, hi, frames, cols):
    chans = lhs.shape[0] // 3
    acc = [None] * frames
    for g0 in range(0, frames, 2):
        count = min(2, frames - g0)
        reach = min(3, g0 + count)
        part = dot(lhs[: reach * chans, k0:k1], stack[lo:hi, g0 * cols : (g0 + count) * cols])
        for back in range(reach):
            for n in range(count):
                f = g0 + n - back
                if f >= 0:
                    piece = part[back * chans : (back + 1) * chans, n * cols : (n + 1) * cols]
                    acc[f] = piece if acc[f] is None else acc[f] + piece
    return acc


def finish(act_grad, feat, cot, gain, shift):
    values, scale, normed = normalized(feat, gain, shift)
    sig = 1.0 / (1.0 + jnp.exp(-normed))
    norm_grad = act_grad * sig * (1.0 + normed * (1.0 - sig)) * gain
    inner = jnp.sum(norm_grad * values, axis=0, keepdims=True) * (1.0 / values.shape[0])
    return cot.astype(jnp.float32) + scale * norm_grad - values * (scale * scale * scale * inner)


def put_row(out, r, grads, packed):
    frames = len(grads)
    if packed:
        dests = out.shape[0]
        cols = grads[0].shape[1]
        wide = [g[:128] for g in grads]
        for f in range(0, frames, 2):
            wide.append(jnp.concatenate([grads[f][128:], grads[f + 1][128:]], axis=0))
        tiles = [jnp.transpose(w).reshape(dests, cols // dests, 128) for w in wide]
        out[:, r] = jnp.concatenate(tiles, axis=1).astype(jnp.bfloat16)
    else:
        for f in range(frames):
            out[f, r] = jnp.transpose(grads[f]).astype(jnp.bfloat16)


def fetch(pairs, sems):
    copies = [pltpu.make_async_copy(s, d, sems.at[n]) for n, (s, d) in enumerate(pairs)]
    for c in copies:
        c.start()
    return copies


def rows_sent(rows):
    inner = jnp.where(lax.rem(lax.axis_index("slab"), 2) == 0, rows - 1, 0)
    return inner, rows - 1 - inner


def staging_kernel(cot, to_outer, to_inner, sems):
    inner, outer = rows_sent(cot.shape[1])
    for c in fetch([(cot.at[:, inner], to_inner), (cot.at[:, outer], to_outer)], sems):
        c.wait()


def backward_local_kernel(
    cot, feat, cache, kern, gain_in, shift_in,
    middle, to_outer, partial, weights,
    stack, tail, edge_sems, *, packed,
):
    frames, rows, chans, cols = cot.shape
    past = cache.shape[0]
    block = 3 * chans
    _, outer = rows_sent(rows)
    written = fetch(
        [(feat.at[:, outer], to_outer.at[pl.ds(past, frames)]), (cache.at[:, outer], to_outer.at[pl.ds(0, past)])],
        edge_sems,
    )
    @pl.loop(0, rows)
    def _(p):
        for f in range(frames):
            shifted_to(stack, pl.multiple_of(p * block, 64), f * cols, cot[f, p], (1, 0, -1))

    for t in range(3):
        taps = [kern[t, 2 - d, j] for d in range(3) for j in range(3)]
        rows_of_t = pl.ds((2 - t) * chans, chans)
        side_by_side(weights.at[rows_of_t], taps)
        side_by_side(tail.at[rows_of_t], taps[3:])
    gain = column(gain_in[...], cols)
    shift = column(shift_in[...], cols)
    for r in range(rows):
        d0, n, first = local_taps(r, rows)
        lhs = tail if d0 == 1 else weights
        acc = grad_sum(lhs, 0, n * block, stack, first * block, (first + n) * block, frames, cols)
        if n == 3:
            grads = [finish(acc[f], feat[f, r], cot[f, r], gain, shift) for f in range(frames)]
            put_row(middle, r - 1, grads, packed)
        else:
            for f in range(frames):
                partial[min(r, 1), f] = acc[f]
    for c in written:
        c.wait()


def backward_edge_kernel(
    cot, outer, inner, feat, partial, weights, gain_in, shift_in, middle, out, stack, sent, out_sem, *, packed
):
    frames, rows, chans, cols = cot.shape
    block = 3 * chans
    written = []
    if rows > 2:
        written.append(pltpu.make_async_copy(middle, out.at[:, 1 : rows - 1], out_sem.at[4]))
        written[0].start()
    slot = jnp.where(lax.rem(lax.axis_index("slab"), 2) == 0, 1, 0)
    for f in range(frames):
        shifted_to(stack.at[slot], 0, f * cols, inner[f], (1, 0, -1))
        shifted_to(stack.at[1 - slot], 0, f * cols, outer[f], (1, 0, -1))
    gain = column(gain_in[...], cols)
    shift = column(shift_in[...], cols)
    for edge, r in enumerate(sorted({0, rows - 1})):
        acc = [partial[edge, f] for f in range(frames)]
        for d, there in ((0, r == 0), (2, r == rows - 1)):
            if there:
                more = grad_sum(weights, d * block, (d + 1) * block, stack.at[d // 2], 0, block, frames, cols)
                acc = [a + b for a, b in zip(acc, more)]
        grads = [finish(acc[f], feat[f, r], cot[f, r], gain, shift) for f in range(frames)]
        put_row(sent, edge, grads, packed)
        half = out.shape[0] // 2
        for n, part in enumerate((pl.ds(0, half), pl.ds(half, half))):
            written.append(pltpu.make_async_copy(sent.at[part, edge], out.at[part, r], out_sem.at[2 * edge + n]))
            written[-1].start()
    for c in written:
        c.wait()


def conv_sum(lhs_of, stack, lo, hi, frames, cols):
    acc = []
    for f0 in range(0, frames, 2):
        count = min(2, frames - f0)
        total = None
        for t in range(3):
            part = dot(lhs_of(t), stack[lo:hi, (f0 + t) * cols : (f0 + t + count) * cols])
            total = part if total is None else total + part
        acc += [total[:, n * cols : (n + 1) * cols] for n in range(count)]
    return acc


def activated(x, gain, shift):
    _, _, normed = normalized(x, gain, shift)
    return normed / (1.0 + jnp.exp(-normed))


def forward_local_kernel(
    feat, cache, kern, gain_in, shift_in, bias_in,
    out, to_inner, partial, weights, stack, tail, ready, out_sem, edge_sems,
):
    frames, rows, chans, cols = feat.shape
    past = cache.shape[0]
    block = 3 * chans
    gain = column(gain_in[...], cols)
    shift = column(shift_in[...], cols)
    bias = column(bias_in[...], cols)
    inner, _ = rows_sent(rows)
    written = fetch(
        [(feat.at[:, inner], to_inner.at[pl.ds(past, frames)]), (cache.at[:, inner], to_inner.at[pl.ds(0, past)])],
        edge_sems,
    )
    for t in range(3):
        whole = jnp.transpose(kern[t].reshape(3 * block, chans))
        weights[t] = whole
        tail[t] = whole[:, block:]
    for p in range(rows):
        for f in range(past):
            shifted_to(stack, p * block, f * cols, cache[f, p], (-1, 0, 1))
        for f in range(frames):
            act = activated(feat[f, p], gain, shift).astype(jnp.bfloat16)
            shifted_to(stack, p * block, (past + f) * cols, act, (-1, 0, 1))
    for r in list(range(1, rows - 1)) + sorted({0, rows - 1}):
        d0, n, first = local_taps(r, rows)

        def lhs_of(t):
            if d0 == 1:
                return tail[t, :, : n * block]
            return weights[t, :, : n * block]

        acc = conv_sum(lhs_of, stack, first * block, (first + n) * block, frames, cols)
        decoded = [feat[f, r].astype(jnp.float32) + acc[f] + bias for f in range(frames)]
        if n == 3:
            for f in range(frames):
                ready[f, r - 1] = decoded[f].astype(jnp.bfloat16)
            written.append(pltpu.make_async_copy(ready.at[:, r - 1], out.at[:, r], out_sem.at[r - 1]))
            written[-1].start()
        else:
            for f in range(frames):
                partial[min(r, 1), f] = decoded[f]
    for c in written:
        c.wait()


def forward_edge_kernel(
    inner_hbm, outer_hbm, partial, weights, gain_in, shift_in, before, out, inner, outer, stack, ready, sems, out_sem
):
    del before
    rows = out.shape[1]
    frames, chans, cols = partial.shape[1:]
    past = inner.shape[0] - frames
    block = 3 * chans
    arriving = fetch([(inner_hbm, inner), (outer_hbm, outer)], sems)
    index = lax.axis_index("slab")
    slot = jnp.where(lax.rem(index, 2) == 0, 1, 0)
    inside = jnp.logical_and(index > 0, index < lax.axis_size("slab") - 1)
    gain = column(gain_in[...], cols)
    shift = column(shift_in[...], cols)
    for n, (side, to, held) in enumerate(((inner, slot, None), (outer, 1 - slot, inside))):
        arriving[n].wait()
        for f in range(past):
            shifted_to(stack.at[to], 0, f * cols, side[f], (-1, 0, 1))
        for f in range(past, past + frames):
            act = activated(side[f], gain, shift)
            if held is not None:
                act = jnp.where(held, act, 0.0)
            shifted_to(stack.at[to], 0, f * cols, act.astype(jnp.bfloat16), (-1, 0, 1))
    written = []
    for edge, r in enumerate(sorted({0, rows - 1})):
        acc = [partial[edge, f] for f in range(frames)]
        for d, there in ((0, r == 0), (2, r == rows - 1)):
            if there:
                more = conv_sum(
                    lambda t: weights[t, :, d * block : (d + 1) * block], stack.at[d // 2], 0, block, frames, cols
                )
                acc = [a + b for a, b in zip(acc, more)]
        for f in range(frames):
            ready[f, edge] = acc[f].astype(jnp.bfloat16)
        written.append(pltpu.make_async_copy(ready.at[:, edge], out.at[:, r], out_sem.at[edge]))
        written[-1].start()
    for c in written:
        c.wait()


def unpack_kernel(src_hbm, out_hbm, src, out, in_sem, out_sem):
    frames, lines = out.shape[:2]
    parts = in_sem.shape[0]
    step = lines // parts
    spans = [pl.ds(n * step, step) for n in range(parts)]
    arriving = fetch([(src_hbm.at[s], src.at[s]) for s in spans], in_sem)
    leaving = [pltpu.make_async_copy(out.at[:, s], out_hbm.at[:, s], out_sem.at[n]) for n, s in enumerate(spans)]
    for n, s in enumerate(spans):
        arriving[n].wait()
        for f in range(frames):
            out[f, s, :, :128] = src[s, f * 8 : (f + 1) * 8, :]
            low = (frames + f // 2) * 8
            rest = src[s, low : low + 8, :]
            out[f, s, :, 128:] = rest[:, :, :64] if f % 2 == 0 else rest[:, :, 64:]
        leaving[n].start()
    for c in leaving:
        c.wait()


VMEM = functools.partial(pl.BlockSpec, memory_space=pltpu.VMEM)
HBM = functools.partial(pl.BlockSpec, memory_space=pltpu.HBM)


def call(kernel, name, ins, outs, scratch=(), aliases=None, flops=None):
    result = pl.pallas_call(
        kernel,
        out_shape=[pltpu.HBM(o.shape, o.dtype) if where is HBM else o for o, where in outs],
        in_specs=[where() for _, where in ins],
        out_specs=[where() for _, where in outs],
        scratch_shapes=list(scratch),
        input_output_aliases=aliases or {},
        compiler_params=pltpu.CompilerParams(vmem_limit_bytes=24 * 1024 * 1024),
        cost_estimate=flops and pl.CostEstimate(flops=flops, transcendentals=0, bytes_accessed=0),
        name=name,
    )(*[pltpu.with_memory_space_constraint(a, pltpu.HBM) if where is HBM else a for a, where in ins])
    return result[0] if len(outs) == 1 else result


def body(features, time_cache, cotangent, kernel, norm_gain, norm_shift, conv_bias):
    frames, rows, cols, chans = features.shape
    past = time_cache.shape[0]
    slabs = lax.axis_size("slab")
    within = [(i, i ^ 1) for i in range(slabs)]
    across = [(i, i + 1) for i in range(1, slabs - 1, 2)] + [(i + 1, i) for i in range(1, slabs - 1, 2)]
    feat = jnp.swapaxes(features, 2, 3)
    cache = jnp.swapaxes(time_cache, 2, 3)
    cot = jnp.swapaxes(cotangent, 2, 3)
    gain = norm_gain.reshape(1, chans)
    shift = norm_shift.reshape(1, chans)
    bias = conv_bias.reshape(1, chans)
    block = 3 * chans
    edge_rows = min(rows, 2)
    per = cols // slabs
    packed = per % 8 == 0 and frames % 2 == 0 and chans == 192
    bf16 = functools.partial(jax.ShapeDtypeStruct, dtype=jnp.bfloat16)
    vmem16 = functools.partial(pltpu.VMEM, dtype=jnp.bfloat16)
    partial = jax.ShapeDtypeStruct((edge_rows, frames, chans, cols), jnp.float32)
    weights = bf16((3, chans, 3 * block))

    def sent(n):
        return (slabs, n, frames * per * chans // 128, 128) if packed else (frames, n, cols, chans)

    cot_across, cot_in = call(
        staging_kernel,
        "staging",
        [(cot, HBM)],
        [(bf16((frames, chans, cols)), VMEM)] * 2,
        [pltpu.SemaphoreType.DMA((2,))],
        flops=HINT,
    )
    cot_across = lax.ppermute(cot_across, "slab", across)
    cot_in = lax.ppermute(cot_in, "slab", within)
    middle, act_across, part, lhs = call(
        functools.partial(backward_local_kernel, packed=packed),
        "backward_local",
        [(a, VMEM) for a in (cot, feat, cache, kernel, gain, shift)],
        [(bf16(sent(max(rows - 2, 1))), VMEM)]
        + [(bf16((past + frames, chans, cols)), HBM)]
        + [(partial, VMEM), (bf16((3 * chans, 3 * block)), VMEM)],
        [
            vmem16((rows * block, frames * cols)),
            vmem16((3 * chans, 2 * block)),
            pltpu.SemaphoreType.DMA((2,)),
        ],
    )
    act_across = lax.ppermute(act_across, "slab", across)
    grad = call(
        functools.partial(backward_edge_kernel, packed=packed),
        "backward_edge",
        [(a, VMEM) for a in (cot, cot_across, cot_in, feat, part, lhs, gain, shift, middle)],
        [(bf16(sent(rows)), HBM)],
        [vmem16((2, block, frames * cols)), vmem16(sent(edge_rows)), pltpu.SemaphoreType.DMA((5,))],
    )

    if packed:
        moved = lax.all_to_all(grad, "slab", split_axis=0, concat_axis=0, tiled=True)
        moved = moved.reshape(slabs * rows, -1, 128)
        relaid = (frames, slabs * rows, per, chans)
        parts = 2 if slabs * rows % 2 == 0 else 1
        relaid = call(
            unpack_kernel,
            "unpack",
            [(moved, HBM)],
            [(bf16(relaid), HBM)],
            [vmem16(moved.shape), vmem16(relaid), pltpu.SemaphoreType.DMA((parts,)), pltpu.SemaphoreType.DMA((parts,))],
        )
    else:
        relaid = lax.all_to_all(grad, "slab", split_axis=2, concat_axis=1, tiled=True)

    feat_v, kern_v, gain_v, shift_v, _ = lax.optimization_barrier((feat, kernel, gain, shift, grad))
    decoded, act_in, part, lhs = call(
        forward_local_kernel,
        "forward_local",
        [(a, VMEM) for a in (feat_v, cache, kern_v, gain_v, shift_v, bias)],
        [(bf16((frames, rows, chans, cols)), HBM), (bf16((past + frames, chans, cols)), HBM), (partial, VMEM), (weights, VMEM)],
        [
            vmem16((rows * block, (past + frames) * cols)),
            vmem16((3, chans, 2 * block)),
            vmem16((frames, max(rows - 2, 1), chans, cols)),
            pltpu.SemaphoreType.DMA((max(rows - 2, 1),)),
            pltpu.SemaphoreType.DMA((2,)),
        ],
        flops=HINT,
    )
    act_in = lax.ppermute(act_in, "slab", within)
    decoded = call(
        forward_edge_kernel,
        "forward_edge",
        [(act_in, HBM), (act_across, HBM)] + [(a, VMEM) for a in (part, lhs, gain_v, shift_v)] + [(decoded, HBM)],
        [(bf16((frames, rows, chans, cols)), HBM)],
        [
            vmem16((past + frames, chans, cols)),
            vmem16((past + frames, chans, cols)),
            vmem16((2, block, (past + frames) * cols)),
            vmem16((frames, edge_rows, chans, cols)),
            pltpu.SemaphoreType.DMA((2,)),
            pltpu.SemaphoreType.DMA((edge_rows,)),
        ],
        aliases={6: 0},
    )
    return (jnp.swapaxes(decoded, 2, 3), relaid)


def solution(mesh):
    rows = P(None, ("grp", "slab"), None, None)
    return jax.shard_map(
        body,
        mesh=mesh,
        in_specs=(rows, rows, rows, P(), P(), P(), P()),
        out_specs=(rows, P(None, "grp", "slab", None)),
        check_vma=False,
    )
```

```python
import functools

import jax
import jax.numpy as jnp
from jax import lax
from jax.experimental import pallas as pl
from jax.experimental.pallas import tpu as pltpu
from jax.sharding import PartitionSpec as P

EPS = 1e-06
HINT = 10**10


def column(vector, cols):
    return jnp.transpose(jnp.broadcast_to(vector, (cols, vector.shape[-1])))


def shifted_to(dst, row0, lanes, x, order):
    chans, cols = x.shape
    x32 = x.astype(jnp.float32)
    at = lax.broadcasted_iota(jnp.int32, x.shape, 1)
    for n, s in enumerate(order):
        if s == 0:
            seen = x
        elif s == 1:
            seen = jnp.where(at < cols - 1, pltpu.roll(x32, cols - 1, 1), 0.0)
        else:
            seen = jnp.where(at > 0, pltpu.roll(x32, 1, 1), 0.0)
        dst[pl.ds(row0 + n * chans, chans), pl.ds(lanes, cols)] = seen.astype(dst.dtype)


def normalized(x, gain, shift):
    values = x.astype(jnp.float32)
    mean = jnp.sum(values * values, axis=0, keepdims=True) * (1.0 / values.shape[0])
    scale = lax.rsqrt(mean + EPS)
    return values, scale, values * scale * gain + shift


def side_by_side(dst, taps):
    chans = taps[0].shape[0]
    for k in range(0, len(taps), 2):
        pair = taps[k : k + 2]
        dst[:, k * chans : (k + len(pair)) * chans] = pair[0] if len(pair) == 1 else jnp.concatenate(pair, axis=1)


def local_taps(r, rows):
    first = max(r - 1, 0)
    last = min(r + 1, rows - 1)
    return first - (r - 1), last - first + 1, first


def dot(a, b):
    return jnp.dot(a, b, preferred_element_type=jnp.float32)


def grad_sum(lhs, k0, k1, stack, lo, hi, frames, cols):
    chans = lhs.shape[0] // 3
    acc = [None] * frames
    for g0 in range(0, frames, 2):
        count = min(2, frames - g0)
        reach = min(3, g0 + count)
        part = dot(lhs[: reach * chans, k0:k1], stack[lo:hi, g0 * cols : (g0 + count) * cols])
        for back in range(reach):
            for n in range(count):
                f = g0 + n - back
                if f >= 0:
                    piece = part[back * chans : (back + 1) * chans, n * cols : (n + 1) * cols]
                    acc[f] = piece if acc[f] is None else acc[f] + piece
    return acc


def finish(act_grad, feat, cot, gain, shift):
    values, scale, normed = normalized(feat, gain, shift)
    sig = 1.0 / (1.0 + jnp.exp(-normed))
    norm_grad = act_grad * sig * (1.0 + normed * (1.0 - sig)) * gain
    inner = jnp.sum(norm_grad * values, axis=0, keepdims=True) * (1.0 / values.shape[0])
    return cot.astype(jnp.float32) + scale * norm_grad - values * (scale * scale * scale * inner)


def put_row(out, r, grads, packed):
    frames = len(grads)
    if packed:
        dests = out.shape[0]
        cols = grads[0].shape[1]
        wide = [g[:128] for g in grads]
        for f in range(0, frames, 2):
            wide.append(jnp.concatenate([grads[f][128:], grads[f + 1][128:]], axis=0))
        tiles = [jnp.transpose(w).reshape(dests, cols // dests, 128) for w in wide]
        out[:, r] = jnp.concatenate(tiles, axis=1).astype(jnp.bfloat16)
    else:
        for f in range(frames):
            out[f, r] = jnp.transpose(grads[f]).astype(jnp.bfloat16)


def fetch(pairs, sems):
    copies = [pltpu.make_async_copy(s, d, sems.at[n]) for n, (s, d) in enumerate(pairs)]
    for c in copies:
        c.start()
    return copies


def rows_sent(rows):
    inner = jnp.where(lax.rem(lax.axis_index("slab"), 2) == 0, rows - 1, 0)
    return inner, rows - 1 - inner


def staging_kernel(cot, to_outer, to_inner, sems):
    inner, outer = rows_sent(cot.shape[1])
    for c in fetch([(cot.at[:, inner], to_inner), (cot.at[:, outer], to_outer)], sems):
        c.wait()


def backward_local_kernel(
    cot, feat, cache, kern, gain_in, shift_in,
    middle, to_outer, partial, weights,
    stack, tail, edge_sems, *, packed,
):
    frames, rows, chans, cols = cot.shape
    past = cache.shape[0]
    block = 3 * chans
    _, outer = rows_sent(rows)
    written = fetch(
        [(feat.at[:, outer], to_outer.at[pl.ds(past, frames)]), (cache.at[:, outer], to_outer.at[pl.ds(0, past)])],
        edge_sems,
    )
    @pl.loop(0, rows)
    def _(p):
        for f in range(frames):
            shifted_to(stack, pl.multiple_of(p * block, 64), f * cols, cot[f, p], (1, 0, -1))

    for t in range(3):
        taps = [kern[t, 2 - d, j] for d in range(3) for j in range(3)]
        rows_of_t = pl.ds((2 - t) * chans, chans)
        side_by_side(weights.at[rows_of_t], taps)
        side_by_side(tail.at[rows_of_t], taps[3:])
    gain = column(gain_in[...], cols)
    shift = column(shift_in[...], cols)
    for r in range(rows):
        d0, n, first = local_taps(r, rows)
        lhs = tail if d0 == 1 else weights
        acc = grad_sum(lhs, 0, n * block, stack, first * block, (first + n) * block, frames, cols)
        if n == 3:
            grads = [finish(acc[f], feat[f, r], cot[f, r], gain, shift) for f in range(frames)]
            put_row(middle, r - 1, grads, packed)
        else:
            for f in range(frames):
                partial[min(r, 1), f] = acc[f]
    for c in written:
        c.wait()


def backward_edge_kernel(
    cot, outer, inner, feat, partial, weights, gain_in, shift_in, middle, out, stack, sent, out_sem, *, packed
):
    frames, rows, chans, cols = cot.shape
    block = 3 * chans
    written = []
    if rows > 2:
        written.append(pltpu.make_async_copy(middle, out.at[:, 1 : rows - 1], out_sem.at[4]))
        written[0].start()
    slot = jnp.where(lax.rem(lax.axis_index("slab"), 2) == 0, 1, 0)
    for f in range(frames):
        shifted_to(stack.at[slot], 0, f * cols, inner[f], (1, 0, -1))
        shifted_to(stack.at[1 - slot], 0, f * cols, outer[f], (1, 0, -1))
    gain = column(gain_in[...], cols)
    shift = column(shift_in[...], cols)
    for edge, r in enumerate(sorted({0, rows - 1})):
        acc = [partial[edge, f] for f in range(frames)]
        for d, there in ((0, r == 0), (2, r == rows - 1)):
            if there:
                more = grad_sum(weights, d * block, (d + 1) * block, stack.at[d // 2], 0, block, frames, cols)
                acc = [a + b for a, b in zip(acc, more)]
        grads = [finish(acc[f], feat[f, r], cot[f, r], gain, shift) for f in range(frames)]
        put_row(sent, edge, grads, packed)
        half = out.shape[0] // 2
        for n, part in enumerate((pl.ds(0, half), pl.ds(half, half))):
            written.append(pltpu.make_async_copy(sent.at[part, edge], out.at[part, r], out_sem.at[2 * edge + n]))
            written[-1].start()
    for c in written:
        c.wait()


def conv_sum(lhs_of, stack, lo, hi, frames, cols):
    acc = []
    for f0 in range(0, frames, 2):
        count = min(2, frames - f0)
        total = None
        for t in range(3):
            part = dot(lhs_of(t), stack[lo:hi, (f0 + t) * cols : (f0 + t + count) * cols])
            total = part if total is None else total + part
        acc += [total[:, n * cols : (n + 1) * cols] for n in range(count)]
    return acc


def activated(x, gain, shift):
    _, _, normed = normalized(x, gain, shift)
    return normed / (1.0 + jnp.exp(-normed))


def forward_local_kernel(
    feat, cache, kern, gain_in, shift_in, bias_in,
    out, to_inner, partial, weights, stack, tail, ready, out_sem, edge_sems,
):
    frames, rows, chans, cols = feat.shape
    past = cache.shape[0]
    block = 3 * chans
    gain = column(gain_in[...], cols)
    shift = column(shift_in[...], cols)
    bias = column(bias_in[...], cols)
    inner, _ = rows_sent(rows)
    written = fetch(
        [(feat.at[:, inner], to_inner.at[pl.ds(past, frames)]), (cache.at[:, inner], to_inner.at[pl.ds(0, past)])],
        edge_sems,
    )
    for t in range(3):
        whole = jnp.transpose(kern[t].reshape(3 * block, chans))
        weights[t] = whole
        tail[t] = whole[:, block:]
    for p in range(rows):
        for f in range(past):
            shifted_to(stack, p * block, f * cols, cache[f, p], (-1, 0, 1))
        for f in range(frames):
            act = activated(feat[f, p], gain, shift).astype(jnp.bfloat16)
            shifted_to(stack, p * block, (past + f) * cols, act, (-1, 0, 1))
    for r in list(range(1, rows - 1)) + sorted({0, rows - 1}):
        d0, n, first = local_taps(r, rows)

        def lhs_of(t):
            if d0 == 1:
                return tail[t, :, : n * block]
            return weights[t, :, : n * block]

        acc = conv_sum(lhs_of, stack, first * block, (first + n) * block, frames, cols)
        decoded = [feat[f, r].astype(jnp.float32) + acc[f] + bias for f in range(frames)]
        if n == 3:
            for f in range(frames):
                ready[f, r - 1] = decoded[f].astype(jnp.bfloat16)
            written.append(pltpu.make_async_copy(ready.at[:, r - 1], out.at[:, r], out_sem.at[r - 1]))
            written[-1].start()
        else:
            for f in range(frames):
                partial[min(r, 1), f] = decoded[f]
    for c in written:
        c.wait()


def forward_edge_kernel(
    inner_hbm, outer_hbm, partial, weights, gain_in, shift_in, before, out, inner, outer, stack, ready, sems, out_sem
):
    del before
    rows = out.shape[1]
    frames, chans, cols = partial.shape[1:]
    past = inner.shape[0] - frames
    block = 3 * chans
    arriving = fetch([(inner_hbm, inner), (outer_hbm, outer)], sems)
    index = lax.axis_index("slab")
    slot = jnp.where(lax.rem(index, 2) == 0, 1, 0)
    inside = jnp.logical_and(index > 0, index < lax.axis_size("slab") - 1)
    gain = column(gain_in[...], cols)
    shift = column(shift_in[...], cols)
    for n, (side, to, held) in enumerate(((inner, slot, None), (outer, 1 - slot, inside))):
        arriving[n].wait()
        for f in range(past):
            shifted_to(stack.at[to], 0, f * cols, side[f], (-1, 0, 1))
        for f in range(past, past + frames):
            act = activated(side[f], gain, shift)
            if held is not None:
                act = jnp.where(held, act, 0.0)
            shifted_to(stack.at[to], 0, f * cols, act.astype(jnp.bfloat16), (-1, 0, 1))
    written = []
    for edge, r in enumerate(sorted({0, rows - 1})):
        acc = [partial[edge, f] for f in range(frames)]
        for d, there in ((0, r == 0), (2, r == rows - 1)):
            if there:
                more = conv_sum(
                    lambda t: weights[t, :, d * block : (d + 1) * block], stack.at[d // 2], 0, block, frames, cols
                )
                acc = [a + b for a, b in zip(acc, more)]
        for f in range(frames):
            ready[f, edge] = acc[f].astype(jnp.bfloat16)
        written.append(pltpu.make_async_copy(ready.at[:, edge], out.at[:, r], out_sem.at[edge]))
        written[-1].start()
    for c in written:
        c.wait()


def unpack_kernel(src_hbm, out_hbm, src, out, in_sem, out_sem):
    frames, lines = out.shape[:2]
    parts = in_sem.shape[0]
    step = lines // parts
    spans = [pl.ds(n * step, step) for n in range(parts)]
    arriving = fetch([(src_hbm.at[s], src.at[s]) for s in spans], in_sem)
    leaving = [pltpu.make_async_copy(out.at[:, s], out_hbm.at[:, s], out_sem.at[n]) for n, s in enumerate(spans)]
    for n, s in enumerate(spans):
        arriving[n].wait()
        for f in range(frames):
            out[f, s, :, :128] = src[s, f * 8 : (f + 1) * 8, :]
            low = (frames + f // 2) * 8
            rest = src[s, low : low + 8, :]
            out[f, s, :, 128:] = rest[:, :, :64] if f % 2 == 0 else rest[:, :, 64:]
        leaving[n].start()
    for c in leaving:
        c.wait()


VMEM = functools.partial(pl.BlockSpec, memory_space=pltpu.VMEM)
HBM = functools.partial(pl.BlockSpec, memory_space=pltpu.HBM)


def call(kernel, name, ins, outs, scratch=(), aliases=None, flops=None):
    result = pl.pallas_call(
        kernel,
        out_shape=[pltpu.HBM(o.shape, o.dtype) if where is HBM else o for o, where in outs],
        in_specs=[where() for _, where in ins],
        out_specs=[where() for _, where in outs],
        scratch_shapes=list(scratch),
        input_output_aliases=aliases or {},
        compiler_params=pltpu.CompilerParams(vmem_limit_bytes=24 * 1024 * 1024),
        cost_estimate=flops and pl.CostEstimate(flops=flops, transcendentals=0, bytes_accessed=0),
        name=name,
    )(*[pltpu.with_memory_space_constraint(a, pltpu.HBM) if where is HBM else a for a, where in ins])
    return result[0] if len(outs) == 1 else result


def body(features, time_cache, cotangent, kernel, norm_gain, norm_shift, conv_bias):
    frames, rows, cols, chans = features.shape
    past = time_cache.shape[0]
    slabs = lax.axis_size("slab")
    within = [(i, i ^ 1) for i in range(slabs)]
    across = [(i, i + 1) for i in range(1, slabs - 1, 2)] + [(i + 1, i) for i in range(1, slabs - 1, 2)]
    feat = jnp.swapaxes(features, 2, 3)
    cache = jnp.swapaxes(time_cache, 2, 3)
    cot = jnp.swapaxes(cotangent, 2, 3)
    gain = norm_gain.reshape(1, chans)
    shift = norm_shift.reshape(1, chans)
    bias = conv_bias.reshape(1, chans)
    block = 3 * chans
    edge_rows = min(rows, 2)
    per = cols // slabs
    packed = per % 8 == 0 and frames % 2 == 0 and chans == 192
    bf16 = functools.partial(jax.ShapeDtypeStruct, dtype=jnp.bfloat16)
    vmem16 = functools.partial(pltpu.VMEM, dtype=jnp.bfloat16)
    partial = jax.ShapeDtypeStruct((edge_rows, frames, chans, cols), jnp.float32)
    weights = bf16((3, chans, 3 * block))

    def sent(n):
        return (slabs, n, frames * per * chans // 128, 128) if packed else (frames, n, cols, chans)

    cot_across, cot_in = call(
        staging_kernel,
        "staging",
        [(cot, HBM)],
        [(bf16((frames, chans, cols)), VMEM)] * 2,
        [pltpu.SemaphoreType.DMA((2,))],
        flops=HINT,
    )
    cot_across = lax.ppermute(cot_across, "slab", across)
    cot_in = lax.ppermute(cot_in, "slab", within)
    middle, act_across, part, lhs = call(
        functools.partial(backward_local_kernel, packed=packed),
        "backward_local",
        [(a, VMEM) for a in (cot, feat, cache, kernel, gain, shift)],
        [(bf16(sent(max(rows - 2, 1))), VMEM)]
        + [(bf16((past + frames, chans, cols)), HBM)]
        + [(partial, VMEM), (bf16((3 * chans, 3 * block)), VMEM)],
        [
            vmem16((rows * block, frames * cols)),
            vmem16((3 * chans, 2 * block)),
            pltpu.SemaphoreType.DMA((2,)),
        ],
    )
    act_across = lax.ppermute(act_across, "slab", across)
    grad = call(
        functools.partial(backward_edge_kernel, packed=packed),
        "backward_edge",
        [(a, VMEM) for a in (cot, cot_across, cot_in, feat, part, lhs, gain, shift, middle)],
        [(bf16(sent(rows)), HBM)],
        [vmem16((2, block, frames * cols)), vmem16(sent(edge_rows)), pltpu.SemaphoreType.DMA((5,))],
    )

    if packed:
        moved = lax.all_to_all(grad, "slab", split_axis=0, concat_axis=0, tiled=True)
        moved = moved.reshape(slabs * rows, -1, 128)
        relaid = (frames, slabs * rows, per, chans)
        parts = 4 if slabs * rows % 4 == 0 else 1
        relaid = call(
            unpack_kernel,
            "unpack",
            [(moved, HBM)],
            [(bf16(relaid), HBM)],
            [vmem16(moved.shape), vmem16(relaid), pltpu.SemaphoreType.DMA((parts,)), pltpu.SemaphoreType.DMA((parts,))],
        )
    else:
        relaid = lax.all_to_all(grad, "slab", split_axis=2, concat_axis=1, tiled=True)

    feat_v, kern_v, gain_v, shift_v, _ = lax.optimization_barrier((feat, kernel, gain, shift, grad))
    decoded, act_in, part, lhs = call(
        forward_local_kernel,
        "forward_local",
        [(a, VMEM) for a in (feat_v, cache, kern_v, gain_v, shift_v, bias)],
        [(bf16((frames, rows, chans, cols)), HBM), (bf16((past + frames, chans, cols)), HBM), (partial, VMEM), (weights, VMEM)],
        [
            vmem16((rows * block, (past + frames) * cols)),
            vmem16((3, chans, 2 * block)),
            vmem16((frames, max(rows - 2, 1), chans, cols)),
            pltpu.SemaphoreType.DMA((max(rows - 2, 1),)),
            pltpu.SemaphoreType.DMA((2,)),
        ],
        flops=HINT,
    )
    act_in = lax.ppermute(act_in, "slab", within)
    decoded = call(
        forward_edge_kernel,
        "forward_edge",
        [(act_in, HBM), (act_across, HBM)] + [(a, VMEM) for a in (part, lhs, gain_v, shift_v)] + [(decoded, HBM)],
        [(bf16((frames, rows, chans, cols)), HBM)],
        [
            vmem16((past + frames, chans, cols)),
            vmem16((past + frames, chans, cols)),
            vmem16((2, block, (past + frames) * cols)),
            vmem16((frames, edge_rows, chans, cols)),
            pltpu.SemaphoreType.DMA((2,)),
            pltpu.SemaphoreType.DMA((edge_rows,)),
        ],
        aliases={6: 0},
    )
    return (jnp.swapaxes(decoded, 2, 3), relaid)


def solution(mesh):
    rows = P(None, ("grp", "slab"), None, None)
    return jax.shard_map(
        body,
        mesh=mesh,
        in_specs=(rows, rows, rows, P(), P(), P(), P()),
        out_specs=(rows, P(None, "grp", "slab", None)),
        check_vma=False,
    )
```
